128 devices in a mesh: chan: 4 (over y), space: 32 (over x, z, core).
Axes of the slice: x: 4, y: 4, z: 4, core: 2. Of those that a mesh axis runs over, the one named last changes fastest.
Arguments:
- features: bfloat16 [16384, 512], P('space', 'chan'), may hold values from -6 to 6
- positions: float32 [3, 16384], replicated, may hold values from 0 to 8
- pair_first: int32 [512], P('space'), may hold values from 0 to 127, as said below
- pair_second: int32 [512], P('space'), may hold values from 0 to 127, as said below
- pair_counts: int32 [32], P('space'), may hold values from 1 to 16, 384 in all
- wave_index: int32 [3, 1024], replicated, may hold values from -6 to 6, as said below
- radial_weight: bfloat16 [32, 512], P(None, 'chan'), may hold values from -1 to 1
- smearing: float32 [512], P('chan'), may hold values from 0.1 to 0.6
- mix_weight: bfloat16 [512, 512], P(None, 'chan'), may hold values from -0.25 to 0.25
Outputs:
- updated: bfloat16 [16384, 512], P('space', 'chan')
The draws below stay inside these ranges and needn't reach their ends.
Inputs may be any that keep to these rules, and one draw needn't show every extreme that they name: `pair_first`: slot t belongs to spatial device t // 16; its first block lies on that device, which holds blocks d * 4 onward. `pair_second`: the second blocks of the 16 slots of one spatial device lie on 16 distinct spatial devices. Device d lists its first pair_counts[d] slots; the others are unused. `wave_index`: no wavevector index is the zero vector.
All inputs are finite; a program needn't handle non-finite values.
Results may differ from the reference program's by a relative error of at most 0.0064.
Values may be sent and summed in bfloat16 or wider, within the bound.
A program may use at most 64 MiB of HBM per device.

```python
import math
import jax
import jax.numpy as jnp
import numpy as np
from jax import lax

C = 512
NB = 32
KV = 1024
BLOCK = 128
ATOM_DEV = 512
PAIR_DEV = 16
ATOMS = 16384
SLOTS = 512
N_SPACE = 32


def pair_table(key):
    devices = SLOTS // PAIR_DEV
    per_device = ATOM_DEV // BLOCK
    subkeys = jax.random.split(jax.random.fold_in(key, 7), devices)

    def shuffle(subkey):
        return jax.random.permutation(subkey, devices)
    orders = jax.vmap(shuffle)(subkeys)[:, :PAIR_DEV]
    first_pick = jax.random.randint(jax.random.fold_in(key, 13), (devices, PAIR_DEV), 0, per_device)
    second_pick = jax.random.randint(jax.random.fold_in(key, 17), (devices, PAIR_DEV), 0, per_device)
    owners = jnp.arange(devices, dtype=jnp.int32)[:, None]
    first = (owners * per_device + first_pick).reshape(-1).astype(jnp.int32)
    second = (orders.astype(jnp.int32) * per_device + second_pick).reshape(-1).astype(jnp.int32)
    return (first, second)


def draw_pair_first(key, part):
    return pair_table(key)[0]


def draw_pair_second(key, part):
    return pair_table(key)[1]


def draw_wave_index(key, part):
    values = jax.random.randint(jax.random.fold_in(key, 29), (3, KV), -6, 7)
    empty = jnp.all(values == 0, axis=0)
    head = jnp.where(empty, 1, values[0])
    return jnp.concatenate([head[None, :], values[1:]], axis=0).astype(jnp.int32)


def level_of(rng, extent, cuts, low, top_value):
    level, own = 1.0, jax.random.fold_in(rng, 6)
    for position, blocks in cuts:
        draws = jnp.exp(jax.random.uniform(jax.random.fold_in(own, position), (blocks,), jnp.float32, low / len(cuts), top_value / len(cuts)))
        level = level * jnp.repeat(draws, extent[position] // blocks).reshape([-1 if axis == position else 1 for axis in range(len(extent))])
    return level


def split_up(amount, total, most, skew):
    portions = [(1 << 20) // math.isqrt(rank ** skew) + 1 for rank in range(2, amount + 1)]
    rest, given = total - most - (amount - 1), [1] * (amount - 1)
    while rest > 0:
        free = [i for i in range(amount - 1) if given[i] < most]
        whole, remaining = sum([portions[i] for i in free]), rest
        for i in free:
            more = min(most - given[i], max(1, remaining * portions[i] // whole), rest)
            given[i] = given[i] + more
            rest = rest - more
    return np.array([most] + given)


def uneven_parts(own_key, amount, total, reach, lean):
    if amount == 2:
        one = jax.random.randint(own_key, (), max(1, total - reach), min(reach, total - 1) + 1)
        return jnp.stack([one, total - one])
    lengths = jnp.asarray(split_up(amount, total, reach, lean), jnp.int32)
    pairs = (amount - 1) // 2
    donor, receiver = lengths[1:1 + 2 * pairs:2], lengths[2:2 + 2 * pairs:2]
    margin = jnp.minimum(donor - 1, reach - receiver)
    moved = jax.random.randint(jax.random.fold_in(own_key, 1), (pairs,), 0, 1 << 20) % (margin + 1)
    lengths = lengths.at[1:1 + 2 * pairs:2].set(donor - moved).at[2:2 + 2 * pairs:2].set(receiver + moved)
    return lengths[jax.random.permutation(jax.random.fold_in(own_key, 2), amount)]


def gaussian(rng, extent, deviation, bound, shards=(), held_as=jnp.bfloat16):
    result = jax.random.normal(rng, extent, jnp.float32) * deviation
    if len(shards) > 0:
        result = level_of(rng, extent, shards, -0.22, 0.18) * result
    return jnp.clip(result, min=-bound, max=bound).astype(held_as)


def setup_inputs(seed: int = 0) -> dict:
    key_of = jax.random.split(jax.random.key(seed), 10)
    return {
        "features": gaussian(key_of[0], (ATOMS, C), 1.0, 6.0, ((0, 32), (1, 4))),
        "positions": jnp.clip(jax.random.uniform(key_of[1], (3, ATOMS), jnp.float32, 0.0, 8.0), 0.0, 8.0),
        "pair_first": draw_pair_first(jax.random.fold_in(key_of[9], 71), 0),
        "pair_second": draw_pair_second(jax.random.fold_in(key_of[9], 71), 0),
        "pair_counts": uneven_parts(key_of[4], N_SPACE, N_SPACE * PAIR_DEV * 3 // 4, PAIR_DEV, 2).astype(jnp.int32),
        "wave_index": draw_wave_index(jax.random.fold_in(key_of[9], 71), 0),
        "radial_weight": gaussian(key_of[6], (NB, C), NB ** -0.5, 1.0, ((1, 4),)),
        "smearing": jnp.clip(jnp.exp(math.log(0.6) - 1.7917595 * jax.random.uniform(key_of[7], (C,), jnp.float32) ** level_of(key_of[7], (C,), ((0, 4),), -0.2, 0.2)), 0.1, 0.6),
        "mix_weight": gaussian(key_of[8], (C, C), C ** -0.5, 0.25, ((1, 4),)),
    }


box_side = 8.0
radial_scale = 0.25
two_pi = 6.283185307179586

def pair_messages(own_pos, other_pos, own_rows, other_rows, weight):
    offsets = other_pos[:, None, :] - own_pos[:, :, None]
    offsets = offsets - box_side * jnp.floor(offsets / box_side + 0.5)
    distance = jnp.sqrt(lax.optimization_barrier(jnp.sum(offsets * offsets, axis=0)))
    bases = weight.shape[0]
    radial_reach = 0.5 * box_side * jnp.sqrt(jnp.float32(3.0))
    centers = jnp.arange(bases, dtype=jnp.float32) * (radial_reach / (bases - 1))
    spread = 1.5 * radial_reach / (bases - 1)
    expand = jnp.exp(-jnp.square((distance[None, :, :] - centers[:, None, None]) / spread))
    expand = expand.reshape(bases, -1).astype(jnp.bfloat16)
    filters = lax.dot_general(expand, weight, (((0,), (0,)), ((), ())), preferred_element_type=jnp.float32)
    filters = filters.reshape(own_rows.shape[0], other_rows.shape[0], -1)
    toward_own = jnp.einsum('ijc,jc->ic', filters, other_rows.astype(jnp.float32), precision=lax.Precision.HIGHEST)
    toward_other = jnp.einsum('ijc,ic->jc', filters, own_rows.astype(jnp.float32), precision=lax.Precision.HIGHEST)
    return (toward_own, toward_other)

def add_block(running, extra, block_id):
    start = (block_id * BLOCK).astype(jnp.int32)
    zero_col = jnp.zeros((), jnp.int32)
    current = lax.dynamic_slice(running, (start, zero_col), extra.shape)
    return lax.dynamic_update_slice(running, current + extra, (start, zero_col))

def reference(features, positions, pair_first, pair_second, pair_counts, wave_index, radial_weight, smearing, mix_weight):

    def visit_pair(slot_index, running):
        device_id = slot_index // PAIR_DEV
        listed = slot_index % PAIR_DEV < pair_counts[device_id]
        first_block = pair_first[slot_index].astype(jnp.int32)
        second_block = pair_second[slot_index].astype(jnp.int32)

        def work(state_sum):
            own_rows = lax.dynamic_slice_in_dim(features, first_block * BLOCK, BLOCK, 0)
            other_rows = lax.dynamic_slice_in_dim(features, second_block * BLOCK, BLOCK, 0)
            own_pos = lax.dynamic_slice_in_dim(positions, first_block * BLOCK, BLOCK, 1)
            other_pos = lax.dynamic_slice_in_dim(positions, second_block * BLOCK, BLOCK, 1)
            toward_own, toward_other = pair_messages(own_pos, other_pos, own_rows, other_rows, radial_weight)
            state_sum = add_block(state_sum, toward_own, first_block)
            return add_block(state_sum, toward_other, second_block)
        return lax.cond(listed, work, lambda state_sum: state_sum, running)
    real_sum = lax.fori_loop(0, SLOTS, visit_pair, jnp.zeros((ATOMS, C), jnp.float32))
    phases = two_pi / box_side * lax.dot_general(wave_index.astype(jnp.float32), positions, (((0,), (0,)), ((), ())), precision=lax.Precision.HIGHEST)
    cosines = jnp.cos(phases).astype(jnp.bfloat16)
    sines = jnp.sin(phases).astype(jnp.bfloat16)
    s_cos = jnp.dot(cosines, features, preferred_element_type=jnp.float32)
    s_sin = jnp.dot(sines, features, preferred_element_type=jnp.float32)
    wave_sq = (two_pi / box_side) ** 2 * lax.optimization_barrier(jnp.sum(jnp.square(wave_index.astype(jnp.float32)), axis=0))
    kernel = (4.0 * jnp.pi / wave_sq)[:, None] * jnp.exp(-0.5 * wave_sq[:, None] * jnp.square(smearing)[None, :])
    f_cos = (s_cos * kernel).astype(jnp.bfloat16)
    f_sin = (s_sin * kernel).astype(jnp.bfloat16)
    contract = (((0,), (0,)), ((), ()))
    recip = lax.dot_general(cosines, f_cos, contract, preferred_element_type=jnp.float32)
    recip = recip + lax.dot_general(sines, f_sin, contract, preferred_element_type=jnp.float32)
    recip = recip * (4.0 / jnp.sqrt(jnp.float32(ATOMS * KV)))
    message = (radial_scale * real_sum + recip).astype(jnp.bfloat16)
    mixture = jnp.dot(message, mix_weight, preferred_element_type=jnp.float32)
    return (features.astype(jnp.float32) + mixture).astype(jnp.bfloat16)
```

```python
import functools
import math

import jax
import jax.numpy as jnp
from jax import lax
from jax.experimental import pallas as pl
from jax.experimental.pallas import tpu as pltpu
from jax.sharding import PartitionSpec as P

BLOCK = 128
NX, NZ, NCORE, NCHAN = 4, 4, 2, 4
NSPACE = NX * NZ * NCORE
ROWS = 512
CH = 128
KV = 1024
NB = 32
MESH = pl.DeviceIdType.MESH
VM = pl.BlockSpec(memory_space=pltpu.VMEM)
SM = pl.BlockSpec(memory_space=pltpu.SMEM)

REACH = 4.0 * math.sqrt(3.0)
STEP = REACH / (NB - 1)
SPREAD = 1.5 * STEP
SCALE = math.sqrt(math.log2(math.e)) / SPREAD

SIN_C = (3.14159264, -5.167710084, 2.550077523, -0.5982912856, 0.0776576603)
COS_C = (0.9999999532, -4.934792831, 4.058411353, -1.331876568, 0.2196896111)


def horner(v, coeffs):
    out = coeffs[-1] * v + coeffs[-2]
    for c in coeffs[-3::-1]:
        out = out * v + c
    return out


def cos_sin_turns(t):
    u = t - jnp.floor(t + 0.5)
    v = u * u
    s = u * horner(v, SIN_C)
    c = horner(v, COS_C)
    s2 = s + s
    return (1.0 - s2 * s).astype(jnp.bfloat16), (s2 * c).astype(jnp.bfloat16)


def remote(src, dst, send, recv, space):
    return pltpu.make_async_remote_copy(
        src_ref=src, dst_ref=dst, send_sem=send, recv_sem=recv,
        device_id={"space": space}, device_id_type=MESH,
    )


def place(x, z, core):
    return (lax.rem(x + 2 * NX, NX) * NZ + lax.rem(z + 2 * NZ, NZ)) * NCORE + core


HALF = ROWS // 2
QUART = ROWS // 4
FULL, LO, HI = (0, HALF), (0, QUART), (QUART, QUART)
EVENTS = (
    (0, 0, FULL, 1, 0), (0, 0, FULL, -1, 0), (0, 0, FULL, 0, 1), (0, 0, FULL, 0, -1),
    (-1, 0, LO, 1, 0), (-1, 0, FULL, 0, 1), (-1, 0, FULL, 0, -1),
    (1, 0, HI, -1, 0), (1, 0, FULL, 0, 1), (1, 0, FULL, 0, -1),
    (-2, 0, LO, 0, 1), (-2, 0, LO, 0, -1), (2, 0, HI, 0, 1), (2, 0, HI, 0, -1),
    (0, -1, LO, 0, 1), (0, 1, HI, 0, -1),
    (-1, -1, LO, 0, 1), (-1, 1, HI, 0, -1), (1, -1, LO, 0, 1), (1, 1, HI, 0, -1),
    (-2, -1, LO, 0, 1), (2, 1, HI, 0, -1),
)
AFTER = (
    (0, (4, 5, 6)), (1, (7, 8, 9)), (2, (14,)), (3, (15,)), (4, (10, 11)), (7, (12, 13)),
    (5, (16,)), (6, (17,)), (8, (18,)), (9, (19,)), (10, (20,)), (13, (21,)),
    (11, ()), (12, ()), (14, ()), (15, ()), (16, ()), (17, ()), (18, ()), (19, ()), (20, ()), (21, ()),
)
NEV = len(EVENTS)


def gather_kernel(feat, codes, pos, wcol, smear, g, codes_out, fg,
                  s_acc, gs, gr, cs, cr, ps, pr, fs, fr, ls):
    me = lax.axis_index("space")
    core = lax.rem(me, NCORE)
    chip = me // NCORE
    x, z = chip // NZ, lax.rem(chip, NZ)
    partner = chip * NCORE + (1 - core)

    barrier = pltpu.get_barrier_semaphore()

    @pl.loop(1, NSPACE)
    def _(i):
        pl.semaphore_signal(barrier, inc=1, device_id={"space": lax.rem(me + i, NSPACE)},
                            device_id_type=MESH)
    pl.semaphore_wait(barrier, NSPACE - 1)

    own = pltpu.make_async_copy(feat, g.at[me], ls.at[0])
    own.start()
    own_code = pltpu.make_async_copy(codes.at[me], codes_out.at[me], ls.at[1])
    own_code.start()

    def ev(flow, i):
        da, db, (r0, n), sa, sb = EVENTS[i]
        if flow == 0:
            origin, to = place(x + da, z + db, core), place(x + sa, z + sb, core)
        else:
            origin, to = place(x + db, z + da, core), place(x + sb, z + sa, core)
        rows = pl.ds(flow * HALF + r0, n)
        src = feat.at[rows] if da == 0 and db == 0 else g.at[origin, rows]
        return remote(src, g.at[origin, rows], gs.at[flow, i], gr.at[flow, i], to)

    def code_copy(i):
        to = lax.rem(me + i, NSPACE)
        return remote(codes.at[to], codes_out.at[me], cs.at[i], cr.at[i], to)

    def to_partner(i):
        chip_i = i
        slot = chip_i * NCORE + core
        return remote(g.at[slot], g.at[slot], ps.at[i], pr.at[i], partner)

    for i in range(4):
        for flow in (0, 1):
            ev(flow, i).start()

    @pl.loop(1, NSPACE)
    def _(i):
        code_copy(i).start()

    for i, nxt in AFTER:
        for flow in (0, 1):
            ev(flow, i).wait_recv()
            for j in nxt:
                ev(flow, j).start()
    own.wait()
    own_code.wait()

    @pl.loop(0, NX * NZ)
    def _(i):
        to_partner(i).start()

    @pl.loop(0, NX * NZ)
    def _(i):
        to_partner(i).wait_recv()

    s_acc[...] = jnp.zeros_like(s_acc)
    n0, n1, n2 = (wcol[:, a:a + 1] for a in range(3))

    @pl.loop(0, NSPACE)
    def _(o):
        at = pl.ds(pl.multiple_of(o * ROWS, ROWS), ROWS)
        t = (n0 * pos[0:1, at] + n1 * pos[1:2, at] + n2 * pos[2:3, at]) * 0.125
        c, s = cos_sin_turns(t)
        s_acc[...] += jnp.dot(jnp.concatenate([c, s], 0), g[o], preferred_element_type=jnp.float32)

    q = (2.0 * math.pi / 8.0) ** 2 * (n0 * n0 + n1 * n1 + n2 * n2)
    sm = smear[...]
    kern = (4.0 * math.pi / q) * jnp.exp(-0.5 * q * (sm * sm))
    fg[core, 0, chip] = (s_acc[0:32, :] * kern).astype(jnp.bfloat16)
    fg[core, 1, chip] = (s_acc[32:64, :] * kern).astype(jnp.bfloat16)

    def f_copy(i):
        dx, dz = i // NZ, lax.rem(i, NZ)
        mine = fg.at[core, :, chip]
        return remote(mine, mine, fs.at[i], fr.at[i], place(x + dx, z + dz, core))

    @pl.loop(1, NX * NZ)
    def _(i):
        f_copy(i).start()

    @pl.loop(1, NX * NZ)
    def _(i):
        f_copy(i).wait_recv()

    last = remote(fg.at[core], fg.at[core], fs.at[0], fr.at[0], partner)
    last.start()
    last.wait_recv()

    for i in range(NEV):
        for flow in (0, 1):
            ev(flow, i).wait_send()

    @pl.loop(1, NSPACE)
    def _(i):
        code_copy(i).wait()

    @pl.loop(0, NX * NZ)
    def _(i):
        to_partner(i).wait_send()

    @pl.loop(1, NX * NZ)
    def _(i):
        f_copy(i).wait_send()
    last.wait_send()


def gather_call(feat, codes, pos, wcol, smear):
    dma = pltpu.SemaphoreType.DMA
    return pl.pallas_call(
        gather_kernel,
        out_shape=(
            jax.ShapeDtypeStruct((NSPACE, ROWS, CH), jnp.bfloat16),
            jax.ShapeDtypeStruct((NSPACE, 1, 128), jnp.int32),
            jax.ShapeDtypeStruct((NCORE, 2, NX * NZ, 32, CH), jnp.bfloat16),
        ),
        in_specs=[VM] * 5,
        out_specs=(VM, VM, VM),
        scratch_shapes=[
            pltpu.VMEM((64, CH), jnp.float32),
            dma((2, NEV)), dma((2, NEV)),
            dma((NSPACE,)), dma((NSPACE,)),
            dma((NX * NZ,)), dma((NX * NZ,)),
            dma((NX * NZ,)), dma((NX * NZ,)),
            dma((2,)),
        ],
        compiler_params=pltpu.CompilerParams(collective_id=0, has_side_effects=True),
        name="gather",
    )(feat, codes, pos, wcol, smear)


def pair_kernel(first, second, count, codes, pos, posc, g, w, wave, fg, msg, acc, wb, csb):
    me = lax.axis_index("space")
    acc[...] = jnp.zeros_like(acc)
    for k in range(NB):
        wb[k] = jnp.broadcast_to(w[k:k + 1, :], (16, CH))

    def half(target, source):
        t0 = pl.multiple_of(target * BLOCK, BLOCK)
        q0 = pl.multiple_of(source * BLOCK, BLOCK)
        total = None
        for a in range(3):
            off = pos[a:a + 1, pl.ds(q0, BLOCK)] - posc[pl.ds(t0, BLOCK), a:a + 1]
            off = off - 8.0 * jnp.floor(off * 0.125 + 0.5)
            total = off * off if total is None else total + off * off
        d = jnp.sqrt(total) * SCALE
        f = g[pl.ds(q0, BLOCK), :].reshape(8, 16, CH)
        out = acc[pl.ds(t0, BLOCK), :]
        for k in range(0, NB, 4):
            es, ws = [], []
            for kk in range(k, k + 4):
                a = d - kk * STEP * SCALE
                es.append(jnp.exp2(a * (-a)).astype(jnp.bfloat16))
                ws.append((f * wb[kk][None]).reshape(BLOCK, CH))
            out = out + jnp.dot(jnp.concatenate(es, 1), jnp.concatenate(ws, 0),
                                preferred_element_type=jnp.float32)
        acc[pl.ds(t0, BLOCK), :] = out

    @pl.loop(0, count[0])
    def _(s):
        half(first[s] - me * (ROWS // BLOCK), second[s])

    @pl.loop(0, NSPACE)
    def _(e):
        code = codes[e, 0, 0]

        @pl.when(code > 0)
        def _():
            half((code - 1) // BLOCK, lax.rem(code - 1, BLOCK))

    @pl.loop(0, ROWS // BLOCK)
    def _(b):
        at = pl.ds(pl.multiple_of(b * BLOCK, BLOCK), BLOCK)
        for core in range(NCORE):
            n = [wave[a:a + 1, core * 512:(core + 1) * 512] for a in range(3)]
            t = (posc[at, 0:1] * n[0] + posc[at, 1:2] * n[1] + posc[at, 2:3] * n[2]) * 0.125
            c, s = cos_sin_turns(t)
            csb[:, core * 1024:core * 1024 + 512] = c
            csb[:, core * 1024 + 512:(core + 1) * 1024] = s
        recip = jnp.dot(csb[...], fg[...], preferred_element_type=jnp.float32)
        recip = recip * (4.0 / math.sqrt(16384.0 * KV))
        msg[at, :] = (0.25 * acc[at, :] + recip).astype(jnp.bfloat16)


def pair_call(first, second, count, codes, pos, posc, g, w, wave, fg):
    return pl.pallas_call(
        pair_kernel,
        out_shape=jax.ShapeDtypeStruct((ROWS, CH), jnp.bfloat16),
        in_specs=[SM] * 4 + [VM] * 6,
        out_specs=VM,
        scratch_shapes=[
            pltpu.VMEM((ROWS, CH), jnp.float32),
            pltpu.VMEM((NB, 16, CH), jnp.bfloat16),
            pltpu.VMEM((BLOCK, 2 * KV), jnp.bfloat16),
        ],
        name="pairs",
    )(first, second, count, codes, pos, posc, g, w, wave, fg)


def mix_kernel(msg, mix, feat, out, m, ss, rs, ls):
    me = lax.axis_index("chan")
    up, down = lax.rem(me + 1, NCHAN), lax.rem(me + NCHAN - 1, NCHAN)
    across = lax.rem(me + 2, NCHAN)
    barrier = pltpu.get_barrier_semaphore()
    for peer in (up, down):
        pl.semaphore_signal(barrier, inc=1, device_id={"chan": peer}, device_id_type=MESH)
    pl.semaphore_wait(barrier, 2)

    def copy(i, src, origin, rows, to):
        return pltpu.make_async_remote_copy(
            src_ref=src, dst_ref=m.at[origin, rows], send_sem=ss.at[i], recv_sem=rs.at[i],
            device_id={"chan": to}, device_id_type=MESH)

    lo, hi = pl.ds(0, HALF), pl.ds(HALF, HALF)
    c0 = copy(0, msg.at[lo], me, lo, up)
    c1 = copy(1, msg.at[hi], me, hi, down)
    c2 = copy(2, msg.at[hi], me, hi, up)
    c3 = copy(3, msg.at[lo], me, lo, down)
    c4 = copy(4, m.at[down, lo], down, lo, up)
    c5 = copy(5, m.at[up, hi], up, hi, down)
    c0.start()
    c1.start()
    c2.start()
    c3.start()

    def part(value, origin):
        rows = pl.ds(pl.multiple_of(origin * CH, CH), CH)
        return jnp.dot(value, mix[rows, :], preferred_element_type=jnp.float32)

    total = part(msg[...], me)
    c0.wait_recv()
    c4.start()
    c1.wait_recv()
    c5.start()
    c2.wait_recv()
    total = total + part(m[down], down)
    c3.wait_recv()
    total = total + part(m[up], up)
    c4.wait_recv()
    c5.wait_recv()
    total = total + part(m[across], across)
    out[...] = (feat[...].astype(jnp.float32) + total).astype(jnp.bfloat16)
    for c in (c0, c1, c2, c3, c4, c5):
        c.wait_send()


def mix_call(msg, mix, feat):
    dma = pltpu.SemaphoreType.DMA
    return pl.pallas_call(
        mix_kernel,
        out_shape=jax.ShapeDtypeStruct((ROWS, CH), jnp.bfloat16),
        in_specs=[VM] * 3,
        out_specs=VM,
        scratch_shapes=[pltpu.VMEM((NCHAN, ROWS, CH), jnp.bfloat16), dma((6,)), dma((6,)), dma((1,))],
        compiler_params=pltpu.CompilerParams(collective_id=1, has_side_effects=True),
        name="mix",
    )(msg, mix, feat)


def body(features, positions, pair_first, pair_second, pair_counts, wave_index,
         radial_weight, smearing, mix_weight):
    me = lax.axis_index("space")
    core, chip = lax.rem(me, NCORE), me // NCORE
    slots = pair_first.shape[0]
    listed = jnp.arange(slots) < pair_counts[0]
    partner = pair_second // (ROWS // BLOCK)
    second_local = pair_second - partner * (ROWS // BLOCK)
    code = second_local * BLOCK + pair_first + 1
    match = listed[None, :] & (partner[None, :] == jnp.arange(NSPACE, dtype=jnp.int32)[:, None])
    codes = jnp.sum(jnp.where(match, code[None, :], 0), axis=1)
    codes = jnp.broadcast_to(codes[:, None, None], (NSPACE, 1, 128))
    posc = lax.dynamic_slice_in_dim(positions, me * ROWS, ROWS, 1).T
    wave = wave_index.astype(jnp.float32)
    wcol = lax.dynamic_slice_in_dim(wave, core * 512 + chip * 32, 32, 1).T

    g, codes_in, fg = gather_call(features, codes, positions, wcol, smearing[None, :])
    msg = pair_call(pair_first, pair_second, pair_counts, codes_in, positions, posc,
                    g.reshape(NSPACE * ROWS, CH), radial_weight, wave, fg.reshape(2 * KV, CH))
    return mix_call(msg, mix_weight, features)


def solution(mesh):
    placed = (P("space", "chan"), P(), P("space"), P("space"), P("space"), P(),
              P(None, "chan"), P("chan"), P(None, "chan"))
    return jax.shard_map(
        body, mesh=mesh, in_specs=placed, out_specs=P("space", "chan"), check_vma=False
    )
```

```python
import functools
import math

import jax
import jax.numpy as jnp
from jax import lax
from jax.experimental import pallas as pl
from jax.experimental.pallas import tpu as pltpu
from jax.sharding import PartitionSpec as P

BLOCK = 128
NX, NZ, NCORE, NCHAN = 4, 4, 2, 4
NSPACE = NX * NZ * NCORE
ROWS = 512
CH = 128
KV = 1024
NB = 32
MESH = pl.DeviceIdType.MESH
VM = pl.BlockSpec(memory_space=pltpu.VMEM)
SM = pl.BlockSpec(memory_space=pltpu.SMEM)

REACH = 4.0 * math.sqrt(3.0)
STEP = REACH / (NB - 1)
SPREAD = 1.5 * STEP
SCALE = math.sqrt(math.log2(math.e)) / SPREAD
DELTA = STEP * SCALE
GROUP = 8
PER = ROWS // BLOCK

SIN_C = (3.14159264, -5.167710084, 2.550077523, -0.5982912856, 0.0776576603)
COS_C = (0.9999999532, -4.934792831, 4.058411353, -1.331876568, 0.2196896111)


def horner(v, coeffs):
    out = coeffs[-1] * v + coeffs[-2]
    for c in coeffs[-3::-1]:
        out = out * v + c
    return out


def cos_sin_turns(t):
    u = t - jnp.floor(t + 0.5)
    v = u * u
    s = u * horner(v, SIN_C)
    c = horner(v, COS_C)
    s2 = s + s
    return (1.0 - s2 * s).astype(jnp.bfloat16), (s2 * c).astype(jnp.bfloat16)


def remote(src, dst, send, recv, space):
    return pltpu.make_async_remote_copy(
        src_ref=src, dst_ref=dst, send_sem=send, recv_sem=recv,
        device_id={"space": space}, device_id_type=MESH,
    )


def place(x, z, core):
    return (lax.rem(x + 2 * NX, NX) * NZ + lax.rem(z + 2 * NZ, NZ)) * NCORE + core


HALF = ROWS // 2
QUART = ROWS // 4
FULL, LO, HI = (0, HALF), (0, QUART), (QUART, QUART)
EVENTS = (
    (0, 0, FULL, 1, 0), (0, 0, FULL, -1, 0), (0, 0, FULL, 0, 1), (0, 0, FULL, 0, -1),
    (-1, 0, LO, 1, 0), (-1, 0, FULL, 0, 1), (-1, 0, FULL, 0, -1),
    (1, 0, HI, -1, 0), (1, 0, FULL, 0, 1), (1, 0, FULL, 0, -1),
    (-2, 0, LO, 0, 1), (-2, 0, LO, 0, -1), (2, 0, HI, 0, 1), (2, 0, HI, 0, -1),
    (0, -1, LO, 0, 1), (0, 1, HI, 0, -1),
    (-1, -1, LO, 0, 1), (-1, 1, HI, 0, -1), (1, -1, LO, 0, 1), (1, 1, HI, 0, -1),
    (-2, -1, LO, 0, 1), (2, 1, HI, 0, -1),
)
NEV = len(EVENTS)


def expansion(d):
    out = [None] * NB
    half = GROUP // 2
    for c in range(half, NB, GROUP):
        a, b = d - c * DELTA, c * DELTA - d
        mid = jnp.exp2(a * b)
        up, down = jnp.exp2(a * (2.0 * DELTA)), jnp.exp2(b * (2.0 * DELTA))
        out[c] = mid
        e = mid
        for j in range(1, GROUP - half):
            e = e * up
            out[c + j] = e
        e = mid
        for j in range(1, half + 1):
            e = e * down
            out[c - j] = e
    return [e.astype(jnp.bfloat16) for e in out]


def kernel(feat, first, second, count, first_v, second_v, count_v, pos, wave, weight, smear, mix, out,
           g, codes, codes_in, code_s, fg, cs, acc, posb, posq, wt, wb, s_acc, m,
           gs, gr, ks, kr, ps, pr, fs, fr, ms, mr, ls):
    me = lax.axis_index("space")
    yme = lax.axis_index("chan")
    core = lax.rem(me, NCORE)
    chip = me // NCORE
    x, z = chip // NZ, lax.rem(chip, NZ)
    partner = chip * NCORE + (1 - core)
    yup, ydown = lax.rem(yme + 1, NCHAN), lax.rem(yme + NCHAN - 1, NCHAN)
    yacross = lax.rem(yme + 2, NCHAN)

    barrier = pltpu.get_barrier_semaphore()

    @pl.loop(1, NSPACE)
    def _(i):
        pl.semaphore_signal(barrier, inc=1, device_id={"space": lax.rem(me + i, NSPACE)},
                            device_id_type=MESH)
    for peer in (yup, ydown):
        pl.semaphore_signal(barrier, inc=1, device_id={"chan": peer}, device_id_type=MESH)

    own = pltpu.make_async_copy(feat, g.at[pl.ds(me * PER, PER)], ls.at[0])
    own.start()

    sec = second_v[...]
    sec_dev = sec // PER
    code = (sec - sec_dev * PER) * BLOCK + first_v[...] + 1
    slot = lax.broadcasted_iota(jnp.int32, (NSPACE, 16), 1)
    dev = lax.broadcasted_iota(jnp.int32, (NSPACE, 16), 0)
    match = (slot < count_v[...]) & (sec_dev == dev)
    picked = jnp.sum(jnp.where(match, code, 0), axis=1, keepdims=True)
    codes[...] = jnp.broadcast_to(picked, (NSPACE, BLOCK))[:, None, :]

    for k in range(NB):
        j = k % GROUP - GROUP // 2
        row = weight[k:k + 1, :].astype(jnp.float32) * (2.0 ** (-j * j * DELTA * DELTA))
        wb[k] = jnp.broadcast_to(row, (16, CH)).astype(jnp.bfloat16)

    pl.semaphore_wait(barrier, NSPACE - 1 + 2)

    def ev(flow, i):
        da, db, (r0, n), sa, sb = EVENTS[i]
        if flow == 0:
            origin, to = place(x + da, z + db, core), place(x + sa, z + sb, core)
        else:
            origin, to = place(x + db, z + da, core), place(x + sb, z + sa, core)
        first_row = (flow * HALF + r0) // BLOCK
        blocks = g.at[pl.ds(origin * PER + first_row, n // BLOCK)]
        src = feat.at[pl.ds(first_row, n // BLOCK)] if da == 0 and db == 0 else blocks
        return remote(src, blocks, gs.at[flow, i], gr.at[flow, i], to)

    def code_copy(i):
        to = lax.rem(me + i, NSPACE)
        return remote(codes.at[to], codes_in.at[me], ks.at[i], kr.at[i], to)

    def to_partner(c):
        blocks = g.at[pl.ds((c * NCORE + core) * PER, PER)]
        return remote(blocks, blocks, ps.at[c], pr.at[c], partner)

    def start(*events):
        for i in events:
            for flow in (0, 1):
                ev(flow, i).start()

    def arrived(*events):
        for i in events:
            for flow in (0, 1):
                ev(flow, i).wait_recv()

    def chip_at(dx, dz):
        return lax.rem(x + dx + NX, NX) * NZ + lax.rem(z + dz + NZ, NZ)

    start(0, 1, 2, 3)
    own_out = remote(feat, g.at[pl.ds(me * PER, PER)], ps.at[NX * NZ], pr.at[NX * NZ], partner)
    own_out.start()

    @pl.loop(1, NSPACE)
    def _(i):
        code_copy(i).start()
    own_code = pltpu.make_async_copy(codes.at[me], codes_in.at[me], ls.at[1])
    own_code.start()

    for a in range(3):
        for b in range(PER):
            at = pl.ds(pl.multiple_of(me * ROWS + b * BLOCK, BLOCK), BLOCK)
            posb[a, b] = jnp.broadcast_to(pos[a:a + 1, at], (BLOCK, BLOCK)).T
        at = pl.ds(pl.multiple_of(core * 512 + (chip // 4) * BLOCK, BLOCK), BLOCK)
        wt[a] = jnp.broadcast_to(wave[a:a + 1, at].astype(jnp.float32), (BLOCK, BLOCK)).T

    @pl.loop(0, NSPACE * PER // 8)
    def _(i):
        for j in range(8):
            at = pl.ds(pl.multiple_of(i * 1024 + j * BLOCK, BLOCK), BLOCK)
            posq[i * 8 + j] = pos[:, at]
    acc[...] = jnp.zeros_like(acc)
    s_acc[...] = jnp.zeros_like(s_acc)

    @pl.loop(0, PER)
    def _(b):
        at = pl.ds(pl.multiple_of(b * BLOCK, BLOCK), BLOCK)
        for h in range(NCORE):
            for part in range(2):
                k0 = h * 512 + part * 256
                t = None
                for a in range(3):
                    n = wave[a:a + 1, k0:k0 + 256].astype(jnp.float32)
                    p = posb[a, b]
                    term = jnp.concatenate([p, p], 1) * n
                    t = term if t is None else t + term
                c, s = cos_sin_turns(t * 0.125)
                col = h * 1024 + part * 256
                cs[at, col:col + 256] = c
                cs[at, col + 512:col + 768] = s

    mine = pl.ds(pl.multiple_of(lax.rem(chip, 4) * 32, 32), 32)
    nrow = [wt[a, mine, :] for a in range(3)]

    def distance(target, source):
        total = None
        there = posq[source]
        for a in range(3):
            off = jnp.abs(there[a:a + 1, :] - posb[a, target])
            off = jnp.minimum(off, 8.0 - off)
            total = off * off if total is None else total + off * off
        return jnp.sqrt(total) * SCALE

    def half_pair(target, source, f32_rows):
        es = expansion(distance(target, source))
        f = f32_rows.astype(jnp.bfloat16).reshape(8, 16, CH)
        total = None
        for k in range(0, NB, 4):
            lhs = jnp.concatenate(es[k:k + 4], 1)
            rhs = jnp.concatenate([(f * wb[k + j][None]).reshape(BLOCK, CH) for j in range(4)], 0)
            part = jnp.dot(lhs, rhs, preferred_element_type=jnp.float32)
            total = part if total is None else total + part
        return total

    def add_rows(targets, values):
        for b in range(PER):
            rows = acc[b * BLOCK:(b + 1) * BLOCK, :]
            for target, value in zip(targets, values):
                rows = rows + jnp.where(target == b, value, 0.0)
            acc[b * BLOCK:(b + 1) * BLOCK, :] = rows

    def chip_step(c):
        at = [pl.ds(pl.multiple_of(c * 1024 + i * BLOCK, BLOCK), BLOCK) for i in range(8)]
        blocks = []
        for i in range(8):
            t = nrow[0] * pos[0:1, at[i]] + nrow[1] * pos[1:2, at[i]] + nrow[2] * pos[2:3, at[i]]
            co, si = cos_sin_turns(t * 0.125)
            blocks.append(jnp.concatenate([co, si], 0))
        rows = g[pl.ds(c * NCORE * PER, NCORE * PER)].reshape(NCORE * ROWS, CH)
        s_acc[...] += jnp.dot(jnp.concatenate(blocks, 1), rows, preferred_element_type=jnp.float32)
        targets, values = [], []
        for h in range(NCORE):
            e = c * NCORE + h
            value = code_s[e, 0, 0]
            v = jnp.maximum(value - 1, 0)
            target = v // BLOCK
            source = lax.rem(v, BLOCK)
            local = jnp.where(value > 0, source - e * PER, -1)
            f = None
            for b in range(PER):
                block = g[e * PER + b].astype(jnp.float32)
                block = jnp.where(local == b, block, 0.0)
                f = block if f is None else f + block
            targets.append(target)
            values.append(half_pair(target, source, f))
        add_rows(targets, values)

    def both(c):
        to_partner(c).wait_recv()

    arrived(0, 1, 2, 3)
    start(4, 7, 5, 6, 8, 9, 14, 15)
    near = ((1, 0), (-1, 0), (0, 1), (0, -1))
    for dx, dz in near:
        to_partner(chip_at(dx, dz)).start()

    @pl.loop(1, NSPACE)
    def _(i):
        code_copy(i).wait_recv()
    own_code.wait()
    to_smem = pltpu.make_async_copy(codes_in, code_s, ls.at[2])
    to_smem.start()
    to_smem.wait()
    own.wait()
    own_out.wait_recv()
    arrived(4, 7)
    start(10, 11, 12, 13)
    chip_step(chip)

    def near_step(i):
        sign = 1 - 2 * lax.rem(i, 2)
        along = i // 2
        c = chip_at(sign * (1 - along), sign * along)
        both(c)
        chip_step(c)

    def diag_step(i):
        c = chip_at(1 - 2 * (i // 2), 1 - 2 * lax.rem(i, 2))
        both(c)
        chip_step(c)

    def far_step(i):
        c = chip_at(2 * (1 - i), 2 * i)
        both(c)
        chip_step(c)

    def knight_step(i):
        sign = 1 - 2 * lax.rem(i, 2)
        along = i // 2
        c = chip_at(2 * (1 - along) + sign * along, sign * (1 - along) + 2 * along)
        both(c)
        chip_step(c)

    pl.loop(0, 2)(near_step)
    arrived(5, 6, 8, 9)
    start(16, 17, 18, 19)
    for dx, dz in ((1, 1), (1, -1), (-1, 1), (-1, -1)):
        to_partner(chip_at(dx, dz)).start()
    pl.loop(2, 4)(near_step)
    arrived(10, 13)
    start(20, 21)
    arrived(14, 15)
    for dx, dz in ((2, 0), (0, 2)):
        to_partner(chip_at(dx, dz)).start()
    pl.loop(0, 4)(diag_step)
    arrived(11, 12, 16, 17, 18, 19)
    for dx, dz in ((2, 1), (2, -1), (1, 2), (-1, 2)):
        to_partner(chip_at(dx, dz)).start()
    pl.loop(0, 2)(far_step)
    arrived(20, 21)
    to_partner(chip_at(2, 2)).start()
    pl.loop(0, 4)(knight_step)
    both(chip_at(2, 2))
    chip_step(chip_at(2, 2))

    n = [r[:, 0:1] for r in nrow]
    q = (2.0 * math.pi / 8.0) ** 2 * (n[0] * n[0] + n[1] * n[1] + n[2] * n[2])
    sm = smear[...]
    kern = (4.0 * math.pi / q) * jnp.exp(-0.5 * q * (sm * sm))
    fg[core, 0, chip] = (s_acc[0:32, :] * kern).astype(jnp.bfloat16)
    fg[core, 1, chip] = (s_acc[32:64, :] * kern).astype(jnp.bfloat16)

    def f_copy(i):
        own_f = fg.at[core, :, chip]
        return remote(own_f, own_f, fs.at[i], fr.at[i], lax.rem(me + i, NSPACE))

    @pl.loop(1, NSPACE)
    def _(i):
        f_copy(i).start()

    @pl.loop(0, 8)
    def _(i):
        targets, values = [], []
        for h in range(2):
            s = 2 * i + h
            target, source = lax.rem(first[s], PER), second[s]
            f = g[source].astype(jnp.float32)
            f = jnp.where(s < count[0], f, 0.0)
            targets.append(target)
            values.append(half_pair(target, source, f))
        add_rows(targets, values)

    @pl.loop(1, NSPACE)
    def _(i):
        f_copy(i).wait_recv()

    def message(h):
        at = pl.ds(h * HALF, HALF)
        recip = jnp.dot(cs[at, :], fg[...].reshape(2 * KV, CH), preferred_element_type=jnp.float32)
        recip = recip * (4.0 / math.sqrt(16384.0 * KV))
        m[yme, at, :] = (0.25 * acc[at, :] + recip).astype(jnp.bfloat16)

    def hop(i, origin, rows, to):
        piece = m.at[origin, rows]
        return pltpu.make_async_remote_copy(
            src_ref=piece, dst_ref=piece, send_sem=ms.at[i], recv_sem=mr.at[i],
            device_id={"chan": to}, device_id_type=MESH)

    lo, hi = pl.ds(0, HALF), pl.ds(HALF, HALF)
    c0, c3 = hop(0, yme, lo, yup), hop(3, yme, lo, ydown)
    c1, c2 = hop(1, yme, hi, ydown), hop(2, yme, hi, yup)
    c4, c5 = hop(4, ydown, lo, yup), hop(5, yup, hi, ydown)
    message(0)
    c0.start()
    c3.start()
    message(1)
    c1.start()
    c2.start()

    def mixed(origin):
        rows = pl.ds(pl.multiple_of(origin * CH, CH), CH)
        return jnp.dot(m[origin], mix[rows, :], preferred_element_type=jnp.float32)

    total = feat[...].reshape(ROWS, CH).astype(jnp.float32) + mixed(yme)
    c0.wait_recv()
    c4.start()
    c1.wait_recv()
    c5.start()
    c2.wait_recv()
    total = total + mixed(ydown)
    c3.wait_recv()
    total = total + mixed(yup)
    c4.wait_recv()
    c5.wait_recv()
    out[...] = (total + mixed(yacross)).astype(jnp.bfloat16)

    for i in range(NEV):
        for flow in (0, 1):
            ev(flow, i).wait_send()
    own_out.wait_send()
    for c in (c0, c1, c2, c3, c4, c5):
        c.wait_send()

    @pl.loop(1, NSPACE)
    def _(i):
        code_copy(i).wait_send()
        f_copy(i).wait_send()

    @pl.loop(1, NX * NZ)
    def _(i):
        to_partner(lax.rem(chip + i, NX * NZ)).wait_send()


def body(features, positions, pair_first, pair_second, pair_counts, wave_index,
         radial_weight, smearing, mix_weight):
    dma = pltpu.SemaphoreType.DMA
    bf16, f32 = jnp.bfloat16, jnp.float32
    return pl.pallas_call(
        kernel,
        out_shape=jax.ShapeDtypeStruct((ROWS, CH), bf16),
        in_specs=[VM, SM, SM, SM] + [VM] * 8,
        out_specs=VM,
        scratch_shapes=[
            pltpu.VMEM((NSPACE * PER, BLOCK, CH), bf16),
            pltpu.VMEM((NSPACE, 1, BLOCK), jnp.int32),
            pltpu.VMEM((NSPACE, 1, BLOCK), jnp.int32),
            pltpu.SMEM((NSPACE, 1, BLOCK), jnp.int32),
            pltpu.VMEM((NCORE, 2, NX * NZ, 32, CH), bf16),
            pltpu.VMEM((ROWS, 2 * KV), bf16),
            pltpu.VMEM((ROWS, CH), f32),
            pltpu.VMEM((3, PER, BLOCK, BLOCK), f32),
            pltpu.VMEM((NSPACE * PER, 3, BLOCK), f32),
            pltpu.VMEM((3, BLOCK, BLOCK), f32),
            pltpu.VMEM((NB, 16, CH), bf16),
            pltpu.VMEM((64, CH), f32),
            pltpu.VMEM((NCHAN, ROWS, CH), bf16),
            dma((2, NEV)), dma((2, NEV)),
            dma((NSPACE,)), dma((NSPACE,)),
            dma((NX * NZ + 1,)), dma((NX * NZ + 1,)),
            dma((NSPACE,)), dma((NSPACE,)),
            dma((6,)), dma((6,)),
            dma((3,)),
        ],
        compiler_params=pltpu.CompilerParams(collective_id=0, has_side_effects=True),
        name="layer",
    )(features.reshape(PER, BLOCK, CH), pair_first, pair_second, pair_counts, pair_first[None, :], pair_second[None, :],
      pair_counts[None, :], positions, wave_index, radial_weight, smearing[None, :], mix_weight)


def solution(mesh):
    placed = (P("space", "chan"), P(), P("space"), P("space"), P("space"), P(),
              P(None, "chan"), P("chan"), P(None, "chan"))
    return jax.shard_map(
        body, mesh=mesh, in_specs=placed, out_specs=P("space", "chan"), check_vma=False
    )
```

```python
import functools
import math

import jax
import jax.numpy as jnp
from jax import lax
from jax.experimental import pallas as pl
from jax.experimental.pallas import tpu as pltpu
from jax.sharding import PartitionSpec as P

BLOCK = 128
NX, NZ, NCORE, NCHAN = 4, 4, 2, 4
NSPACE = NX * NZ * NCORE
ROWS = 512
CH = 128
KV = 1024
NB = 32
MESH = pl.DeviceIdType.MESH
VM = pl.BlockSpec(memory_space=pltpu.VMEM)
SM = pl.BlockSpec(memory_space=pltpu.SMEM)

REACH = 4.0 * math.sqrt(3.0)
STEP = REACH / (NB - 1)
SPREAD = 1.5 * STEP
SCALE = math.sqrt(math.log2(math.e)) / SPREAD
DELTA = STEP * SCALE
GROUP = 8
PER = ROWS // BLOCK

SIN_C = (3.14159264, -5.167710084, 2.550077523, -0.5982912856, 0.0776576603)
COS_C = (0.9999999532, -4.934792831, 4.058411353, -1.331876568, 0.2196896111)


def horner(v, coeffs):
    out = coeffs[-1] * v + coeffs[-2]
    for c in coeffs[-3::-1]:
        out = out * v + c
    return out


def cos_sin_turns(t):
    u = t - jnp.floor(t + 0.5)
    v = u * u
    s = u * horner(v, SIN_C)
    c = horner(v, COS_C)
    s2 = s + s
    return (1.0 - s2 * s).astype(jnp.bfloat16), (s2 * c).astype(jnp.bfloat16)


def remote(src, dst, send, recv, space):
    return pltpu.make_async_remote_copy(
        src_ref=src, dst_ref=dst, send_sem=send, recv_sem=recv,
        device_id={"space": space}, device_id_type=MESH,
    )


def place(x, z, core):
    return (lax.rem(x + 2 * NX, NX) * NZ + lax.rem(z + 2 * NZ, NZ)) * NCORE + core


HALF = ROWS // 2
QUART = ROWS // 4
FULL, LO, HI = (0, HALF), (0, QUART), (QUART, QUART)
EVENTS = (
    (0, 0, FULL, 1, 0), (0, 0, FULL, -1, 0), (0, 0, FULL, 0, 1), (0, 0, FULL, 0, -1),
    (-1, 0, LO, 1, 0), (-1, 0, FULL, 0, 1), (-1, 0, FULL, 0, -1),
    (1, 0, HI, -1, 0), (1, 0, FULL, 0, 1), (1, 0, FULL, 0, -1),
    (-2, 0, LO, 0, 1), (-2, 0, LO, 0, -1), (2, 0, HI, 0, 1), (2, 0, HI, 0, -1),
    (0, -1, LO, 0, 1), (0, 1, HI, 0, -1),
    (-1, -1, LO, 0, 1), (-1, 1, HI, 0, -1), (1, -1, LO, 0, 1), (1, 1, HI, 0, -1),
    (-2, -1, LO, 0, 1), (2, 1, HI, 0, -1),
)
NEV = len(EVENTS)


def expansion(d):
    out = [None] * NB
    half = GROUP // 2
    for c in range(half, NB, GROUP):
        a, b = d - c * DELTA, c * DELTA - d
        mid = jnp.exp2(a * b)
        up, down = jnp.exp2(a * (2.0 * DELTA)), jnp.exp2(b * (2.0 * DELTA))
        out[c] = mid
        e = mid
        for j in range(1, GROUP - half):
            e = e * up
            out[c + j] = e
        e = mid
        for j in range(1, half + 1):
            e = e * down
            out[c - j] = e
    return [e.astype(jnp.bfloat16) for e in out]


def kernel(feat, first, second, count, first_v, second_v, count_v, pos, wave, weight, smear, mix, out,
           g, codes, codes_in, code_s, fg, cs, acc, posb, posq, wt, wb, part, parts, m,
           gs, gr, ks, kr, ps, pr, rs, rr, fs, fr, ms, mr, ls):
    me = lax.axis_index("space")
    yme = lax.axis_index("chan")
    core = lax.rem(me, NCORE)
    chip = me // NCORE
    x, z = chip // NZ, lax.rem(chip, NZ)
    partner = chip * NCORE + (1 - core)
    yup, ydown = lax.rem(yme + 1, NCHAN), lax.rem(yme + NCHAN - 1, NCHAN)
    yacross = lax.rem(yme + 2, NCHAN)

    barrier = pltpu.get_barrier_semaphore()

    @pl.loop(1, NSPACE)
    def _(i):
        pl.semaphore_signal(barrier, inc=1, device_id={"space": lax.rem(me + i, NSPACE)},
                            device_id_type=MESH)
    for peer in (yup, ydown):
        pl.semaphore_signal(barrier, inc=1, device_id={"chan": peer}, device_id_type=MESH)

    own = pltpu.make_async_copy(feat, g.at[pl.ds(me * PER, PER)], ls.at[0])
    own.start()

    sec = second_v[...]
    sec_dev = sec // PER
    code = (sec - sec_dev * PER) * BLOCK + first_v[...] + 1
    slot = lax.broadcasted_iota(jnp.int32, (NSPACE, 16), 1)
    dev = lax.broadcasted_iota(jnp.int32, (NSPACE, 16), 0)
    match = (slot < count_v[...]) & (sec_dev == dev)
    picked = jnp.sum(jnp.where(match, code, 0), axis=1, keepdims=True)
    codes[...] = jnp.broadcast_to(picked, (NSPACE, BLOCK))[:, None, :]

    for k in range(NB):
        j = k % GROUP - GROUP // 2
        row = weight[k:k + 1, :].astype(jnp.float32) * (2.0 ** (-j * j * DELTA * DELTA))
        wb[k] = jnp.broadcast_to(row, (16, CH)).astype(jnp.bfloat16)

    pl.semaphore_wait(barrier, NSPACE - 1 + 2)

    def ev(flow, i):
        da, db, (r0, n), sa, sb = EVENTS[i]
        if flow == 0:
            origin, to = place(x + da, z + db, core), place(x + sa, z + sb, core)
        else:
            origin, to = place(x + db, z + da, core), place(x + sb, z + sa, core)
        first_row = (flow * HALF + r0) // BLOCK
        blocks = g.at[pl.ds(origin * PER + first_row, n // BLOCK)]
        src = feat.at[pl.ds(first_row, n // BLOCK)] if da == 0 and db == 0 else blocks
        return remote(src, blocks, gs.at[flow, i], gr.at[flow, i], to)

    def code_copy(i):
        to = lax.rem(me + i, NSPACE)
        return remote(codes.at[to], codes_in.at[me], ks.at[i], kr.at[i], to)

    def to_partner(c):
        blocks = g.at[pl.ds((c * NCORE + core) * PER, PER)]
        return remote(blocks, blocks, ps.at[c], pr.at[c], partner)

    def start(*events):
        for i in events:
            for flow in (0, 1):
                ev(flow, i).start()

    def arrived(*events):
        for i in events:
            for flow in (0, 1):
                ev(flow, i).wait_recv()

    def chip_at(dx, dz):
        return lax.rem(x + dx + NX, NX) * NZ + lax.rem(z + dz + NZ, NZ)

    start(0, 1, 2, 3)
    own_out = remote(feat, g.at[pl.ds(me * PER, PER)], ps.at[NX * NZ], pr.at[NX * NZ], partner)
    own_out.start()

    @pl.loop(1, NSPACE)
    def _(i):
        code_copy(i).start()
    own_code = pltpu.make_async_copy(codes.at[me], codes_in.at[me], ls.at[1])
    own_code.start()

    for a in range(3):
        for b in range(PER):
            at = pl.ds(pl.multiple_of(me * ROWS + b * BLOCK, BLOCK), BLOCK)
            posb[a, b] = jnp.broadcast_to(pos[a:a + 1, at], (BLOCK, BLOCK)).T
        for b in range(KV // BLOCK):
            n = wave[a:a + 1, b * BLOCK:(b + 1) * BLOCK].astype(jnp.float32)
            wt[a, b * BLOCK:(b + 1) * BLOCK, :] = jnp.broadcast_to(n, (BLOCK, BLOCK)).T

    @pl.loop(0, NSPACE * PER // 8)
    def _(i):
        for j in range(8):
            at = pl.ds(pl.multiple_of(i * 1024 + j * BLOCK, BLOCK), BLOCK)
            posq[i * 8 + j] = pos[:, at]
    acc[...] = jnp.zeros_like(acc)

    @pl.loop(0, NX * NZ)
    def _(c):
        rows = []
        for h in range(NCORE):
            ks_at = pl.ds(pl.multiple_of(h * 512 + c * 32, 32), 32)
            n = [wt[a, ks_at, :] for a in range(3)]
            cols = []
            for b in range(PER):
                at = pl.ds(pl.multiple_of(me * ROWS + b * BLOCK, BLOCK), BLOCK)
                t = n[0] * pos[0:1, at] + n[1] * pos[1:2, at] + n[2] * pos[2:3, at]
                co, si = cos_sin_turns(t * 0.125)
                cols.append(jnp.concatenate([co, si], 0))
            rows.append(jnp.concatenate(cols, 1))
        both_parts = jnp.dot(jnp.concatenate(rows, 0), feat[...].reshape(ROWS, CH),
                             preferred_element_type=jnp.float32).astype(jnp.bfloat16)
        part[c * NCORE] = both_parts[0:64]
        part[c * NCORE + 1] = both_parts[64:128]

    parts[me] = part[me]

    def part_copy(i):
        to = lax.rem(me + i, NSPACE)
        return remote(part.at[to], parts.at[me], rs.at[i], rr.at[i], to)

    arrived(0, 1)
    start(4, 5, 6, 7, 8, 9)

    @pl.loop(1, NSPACE)
    def _(i):
        part_copy(i).start()

    arrived(2, 3)
    start(14, 15)
    near = ((1, 0), (-1, 0), (0, 1), (0, -1))
    for dx, dz in near:
        to_partner(chip_at(dx, dz)).start()

    @pl.loop(0, PER)
    def _(b):
        at = pl.ds(pl.multiple_of(b * BLOCK, BLOCK), BLOCK)
        for h in range(NCORE):
            for part in range(2):
                k0 = h * 512 + part * 256
                t = None
                for a in range(3):
                    n = wave[a:a + 1, k0:k0 + 256].astype(jnp.float32)
                    p = posb[a, b]
                    term = jnp.concatenate([p, p], 1) * n
                    t = term if t is None else t + term
                c, s = cos_sin_turns(t * 0.125)
                col = h * 1024 + part * 256
                cs[at, col:col + 256] = c
                cs[at, col + 512:col + 768] = s

    def distance(target, source):
        total = None
        there = posq[source]
        for a in range(3):
            off = jnp.abs(there[a:a + 1, :] - posb[a, target])
            off = jnp.minimum(off, 8.0 - off)
            total = off * off if total is None else total + off * off
        return jnp.sqrt(total) * SCALE

    def half_pair(target, source, f32_rows):
        es = expansion(distance(target, source))
        f = f32_rows.astype(jnp.bfloat16).reshape(8, 16, CH)
        total = None
        for k in range(0, NB, 4):
            lhs = jnp.concatenate(es[k:k + 4], 1)
            rhs = jnp.concatenate([(f * wb[k + j][None]).reshape(BLOCK, CH) for j in range(4)], 0)
            part = jnp.dot(lhs, rhs, preferred_element_type=jnp.float32)
            total = part if total is None else total + part
        return total

    def add_rows(targets, values):
        for b in range(PER):
            rows = acc[b * BLOCK:(b + 1) * BLOCK, :]
            for target, value in zip(targets, values):
                rows = rows + jnp.where(target == b, value, 0.0)
            acc[b * BLOCK:(b + 1) * BLOCK, :] = rows

    def chip_step(c):
        targets, values = [], []
        for h in range(NCORE):
            e = c * NCORE + h
            value = code_s[e, 0, 0]
            v = jnp.maximum(value - 1, 0)
            target = v // BLOCK
            source = lax.rem(v, BLOCK)
            local = jnp.where(value > 0, source - e * PER, -1)
            f = None
            for b in range(PER):
                block = g[e * PER + b].astype(jnp.float32)
                block = jnp.where(local == b, block, 0.0)
                f = block if f is None else f + block
            targets.append(target)
            values.append(half_pair(target, source, f))
        add_rows(targets, values)

    def both(c):
        to_partner(c).wait_recv()

    arrived(4, 7)
    start(10, 11, 12, 13)
    arrived(5, 6, 8, 9)
    start(16, 17, 18, 19)
    for dx, dz in ((1, 1), (1, -1), (-1, 1), (-1, -1)):
        to_partner(chip_at(dx, dz)).start()

    @pl.loop(1, NSPACE)
    def _(i):
        code_copy(i).wait_recv()
    own_code.wait()
    to_smem = pltpu.make_async_copy(codes_in, code_s, ls.at[2])
    to_smem.start()
    to_smem.wait()
    own.wait()
    own_out.wait_recv()
    chip_step(chip)

    def near_step(i):
        sign = 1 - 2 * lax.rem(i, 2)
        along = i // 2
        c = chip_at(sign * (1 - along), sign * along)
        both(c)
        chip_step(c)

    def diag_step(i):
        c = chip_at(1 - 2 * (i // 2), 1 - 2 * lax.rem(i, 2))
        both(c)
        chip_step(c)

    def far_step(i):
        c = chip_at(2 * (1 - i), 2 * i)
        both(c)
        chip_step(c)

    def knight_step(i):
        sign = 1 - 2 * lax.rem(i, 2)
        along = i // 2
        c = chip_at(2 * (1 - along) + sign * along, sign * (1 - along) + 2 * along)
        both(c)
        chip_step(c)

    pl.loop(0, 2)(near_step)
    arrived(10, 13)
    start(20, 21)
    arrived(14, 15)
    for dx, dz in ((2, 0), (0, 2)):
        to_partner(chip_at(dx, dz)).start()
    pl.loop(2, 4)(near_step)

    @pl.loop(1, NSPACE)
    def _(i):
        part_copy(i).wait_recv()
    total = parts[0].astype(jnp.float32)
    for j in range(1, NSPACE):
        total = total + parts[j].astype(jnp.float32)
    mine = pl.ds(pl.multiple_of(core * 512 + chip * 32, 32), 32)
    n = [wt[a, mine, 0:1] for a in range(3)]
    q = (2.0 * math.pi / 8.0) ** 2 * (n[0] * n[0] + n[1] * n[1] + n[2] * n[2])
    sm = smear[...]
    kern = (4.0 * math.pi / q) * jnp.exp(-0.5 * q * (sm * sm))
    fg[core, 0, chip] = (total[0:32, :] * kern).astype(jnp.bfloat16)
    fg[core, 1, chip] = (total[32:64, :] * kern).astype(jnp.bfloat16)

    def f_copy(i):
        own_f = fg.at[core, :, chip]
        return remote(own_f, own_f, fs.at[i], fr.at[i], lax.rem(me + i, NSPACE))

    @pl.loop(1, NSPACE)
    def _(i):
        f_copy(i).start()

    pl.loop(0, 2)(diag_step)
    arrived(11, 12, 16, 17, 18, 19)
    for dx, dz in ((2, 1), (2, -1), (1, 2), (-1, 2)):
        to_partner(chip_at(dx, dz)).start()
    arrived(20, 21)
    to_partner(chip_at(2, 2)).start()
    pl.loop(2, 4)(diag_step)
    pl.loop(0, 2)(far_step)
    pl.loop(0, 4)(knight_step)
    both(chip_at(2, 2))
    chip_step(chip_at(2, 2))

    @pl.loop(1, NSPACE)
    def _(i):
        f_copy(i).wait_recv()

    for b in range(PER):
        at = pl.ds(b * BLOCK, BLOCK)
        recip = jnp.dot(cs[at, :], fg[...].reshape(2 * KV, CH), preferred_element_type=jnp.float32)
        acc[at, :] += recip * (4.0 * 4.0 / math.sqrt(16384.0 * KV))

    @pl.loop(0, 8)
    def _(i):
        targets, values = [], []
        for h in range(2):
            s = 2 * i + h
            target, source = lax.rem(first[s], PER), second[s]
            f = g[source].astype(jnp.float32)
            f = jnp.where(s < count[0], f, 0.0)
            targets.append(target)
            values.append(half_pair(target, source, f))
        add_rows(targets, values)

    def message(h):
        at = pl.ds(h * HALF, HALF)
        m[yme, at, :] = (0.25 * acc[at, :]).astype(jnp.bfloat16)

    def hop(i, origin, rows, to):
        piece = m.at[origin, rows]
        return pltpu.make_async_remote_copy(
            src_ref=piece, dst_ref=piece, send_sem=ms.at[i], recv_sem=mr.at[i],
            device_id={"chan": to}, device_id_type=MESH)

    lo, hi = pl.ds(0, HALF), pl.ds(HALF, HALF)
    c0, c3 = hop(0, yme, lo, yup), hop(3, yme, lo, ydown)
    c1, c2 = hop(1, yme, hi, ydown), hop(2, yme, hi, yup)
    c4, c5 = hop(4, ydown, lo, yup), hop(5, yup, hi, ydown)
    message(0)
    c0.start()
    c3.start()
    message(1)
    c1.start()
    c2.start()

    def mixed(origin):
        rows = pl.ds(pl.multiple_of(origin * CH, CH), CH)
        return jnp.dot(m[origin], mix[rows, :], preferred_element_type=jnp.float32)

    total = feat[...].reshape(ROWS, CH).astype(jnp.float32) + mixed(yme)
    c0.wait_recv()
    c4.start()
    c1.wait_recv()
    c5.start()
    c2.wait_recv()
    total = total + mixed(ydown)
    c3.wait_recv()
    total = total + mixed(yup)
    c4.wait_recv()
    c5.wait_recv()
    out[...] = (total + mixed(yacross)).astype(jnp.bfloat16)

    for i in range(NEV):
        for flow in (0, 1):
            ev(flow, i).wait_send()
    own_out.wait_send()
    for c in (c0, c1, c2, c3, c4, c5):
        c.wait_send()

    @pl.loop(1, NSPACE)
    def _(i):
        code_copy(i).wait_send()
        part_copy(i).wait_send()
        f_copy(i).wait_send()

    @pl.loop(1, NX * NZ)
    def _(i):
        to_partner(lax.rem(chip + i, NX * NZ)).wait_send()


def body(features, positions, pair_first, pair_second, pair_counts, wave_index,
         radial_weight, smearing, mix_weight):
    dma = pltpu.SemaphoreType.DMA
    bf16, f32 = jnp.bfloat16, jnp.float32
    return pl.pallas_call(
        kernel,
        out_shape=jax.ShapeDtypeStruct((ROWS, CH), bf16),
        in_specs=[VM, SM, SM, SM] + [VM] * 8,
        out_specs=VM,
        scratch_shapes=[
            pltpu.VMEM((NSPACE * PER, BLOCK, CH), bf16),
            pltpu.VMEM((NSPACE, 1, BLOCK), jnp.int32),
            pltpu.VMEM((NSPACE, 1, BLOCK), jnp.int32),
            pltpu.SMEM((NSPACE, 1, BLOCK), jnp.int32),
            pltpu.VMEM((NCORE, 2, NX * NZ, 32, CH), bf16),
            pltpu.VMEM((ROWS, 2 * KV), bf16),
            pltpu.VMEM((ROWS, CH), f32),
            pltpu.VMEM((3, PER, BLOCK, BLOCK), f32),
            pltpu.VMEM((NSPACE * PER, 3, BLOCK), f32),
            pltpu.VMEM((3, KV, BLOCK), f32),
            pltpu.VMEM((NB, 16, CH), bf16),
            pltpu.VMEM((NSPACE, 64, CH), bf16),
            pltpu.VMEM((NSPACE, 64, CH), bf16),
            pltpu.VMEM((NCHAN, ROWS, CH), bf16),
            dma((2, NEV)), dma((2, NEV)),
            dma((NSPACE,)), dma((NSPACE,)),
            dma((NX * NZ + 1,)), dma((NX * NZ + 1,)),
            dma((NSPACE,)), dma((NSPACE,)),
            dma((NSPACE,)), dma((NSPACE,)),
            dma((6,)), dma((6,)),
            dma((3,)),
        ],
        compiler_params=pltpu.CompilerParams(collective_id=0, has_side_effects=True),
        name="layer",
    )(features.reshape(PER, BLOCK, CH), pair_first, pair_second, pair_counts, pair_first[None, :], pair_second[None, :],
      pair_counts[None, :], positions, wave_index, radial_weight, smearing[None, :], mix_weight)


def solution(mesh):
    placed = (P("space", "chan"), P(), P("space"), P("space"), P("space"), P(),
              P(None, "chan"), P("chan"), P(None, "chan"))
    return jax.shard_map(
        body, mesh=mesh, in_specs=placed, out_specs=P("space", "chan"), check_vma=False
    )
```

```python
import functools
import math

import jax
import jax.numpy as jnp
from jax import lax
from jax.experimental import pallas as pl
from jax.experimental.pallas import tpu as pltpu
from jax.sharding import PartitionSpec as P

BLOCK = 128
NX, NZ, NCORE, NCHAN = 4, 4, 2, 4
NSPACE = NX * NZ * NCORE
ROWS = 512
CH = 128
KV = 1024
NB = 32
MESH = pl.DeviceIdType.MESH
VM = pl.BlockSpec(memory_space=pltpu.VMEM)
SM = pl.BlockSpec(memory_space=pltpu.SMEM)

REACH = 4.0 * math.sqrt(3.0)
STEP = REACH / (NB - 1)
SPREAD = 1.5 * STEP
SCALE = math.sqrt(math.log2(math.e)) / SPREAD
DELTA = STEP * SCALE
GROUP = 8
PER = ROWS // BLOCK

SIN_C = (3.14159264, -5.167710084, 2.550077523, -0.5982912856, 0.0776576603)
COS_C = (0.9999999532, -4.934792831, 4.058411353, -1.331876568, 0.2196896111)


def horner(v, coeffs):
    out = coeffs[-1] * v + coeffs[-2]
    for c in coeffs[-3::-1]:
        out = out * v + c
    return out


def cos_sin_turns(t):
    u = t - jnp.floor(t + 0.5)
    v = u * u
    s = u * horner(v, SIN_C)
    c = horner(v, COS_C)
    s2 = s + s
    return (1.0 - s2 * s).astype(jnp.bfloat16), (s2 * c).astype(jnp.bfloat16)


def remote(src, dst, send, recv, space):
    return pltpu.make_async_remote_copy(
        src_ref=src, dst_ref=dst, send_sem=send, recv_sem=recv,
        device_id={"space": space}, device_id_type=MESH,
    )


def place(x, z, core):
    return (lax.rem(x + 2 * NX, NX) * NZ + lax.rem(z + 2 * NZ, NZ)) * NCORE + core


HALF = ROWS // 2
QUART = ROWS // 4
FULL, LO, HI = (0, HALF), (0, QUART), (QUART, QUART)
EVENTS = (
    (0, 0, FULL, 1, 0), (0, 0, FULL, -1, 0), (0, 0, FULL, 0, 1), (0, 0, FULL, 0, -1),
    (-1, 0, LO, 1, 0), (-1, 0, FULL, 0, 1), (-1, 0, FULL, 0, -1),
    (1, 0, HI, -1, 0), (1, 0, FULL, 0, 1), (1, 0, FULL, 0, -1),
    (-2, 0, LO, 0, 1), (-2, 0, LO, 0, -1), (2, 0, HI, 0, 1), (2, 0, HI, 0, -1),
    (0, -1, LO, 0, 1), (0, 1, HI, 0, -1),
    (-1, -1, LO, 0, 1), (-1, 1, HI, 0, -1), (1, -1, LO, 0, 1), (1, 1, HI, 0, -1),
    (-2, -1, LO, 0, 1), (2, 1, HI, 0, -1),
)
NEV = len(EVENTS)


def expansion(d):
    out = [None] * NB
    half = GROUP // 2
    for c in range(half, NB, GROUP):
        a, b = d - c * DELTA, c * DELTA - d
        mid = jnp.exp2(a * b)
        up, down = jnp.exp2(a * (2.0 * DELTA)), jnp.exp2(b * (2.0 * DELTA))
        out[c] = mid
        e = mid
        for j in range(1, GROUP - half):
            e = e * up
            out[c + j] = e
        e = mid
        for j in range(1, half + 1):
            e = e * down
            out[c - j] = e
    return [e.astype(jnp.bfloat16) for e in out]


def kernel(feat, first, second, count, first_v, second_v, count_v, pos, wave, weight, smear, mix, out,
           g, codes, codes_in, code_s, fg, cs, acc, posb, posq, wt, wb, s_acc, m,
           gs, gr, ks, kr, ps, pr, fs, fr, ms, mr, ls):
    me = lax.axis_index("space")
    yme = lax.axis_index("chan")
    core = lax.rem(me, NCORE)
    chip = me // NCORE
    x, z = chip // NZ, lax.rem(chip, NZ)
    partner = chip * NCORE + (1 - core)
    yup, ydown = lax.rem(yme + 1, NCHAN), lax.rem(yme + NCHAN - 1, NCHAN)
    yacross = lax.rem(yme + 2, NCHAN)

    barrier = pltpu.get_barrier_semaphore()

    @pl.loop(1, NSPACE)
    def _(i):
        pl.semaphore_signal(barrier, inc=1, device_id={"space": lax.rem(me + i, NSPACE)},
                            device_id_type=MESH)
    for peer in (yup, ydown):
        pl.semaphore_signal(barrier, inc=1, device_id={"chan": peer}, device_id_type=MESH)

    own = pltpu.make_async_copy(feat, g.at[pl.ds(me * PER, PER)], ls.at[0])
    own.start()

    sec = second_v[...]
    sec_dev = sec // PER
    code = (sec - sec_dev * PER) * BLOCK + first_v[...] + 1
    slot = lax.broadcasted_iota(jnp.int32, (NSPACE, 16), 1)
    dev = lax.broadcasted_iota(jnp.int32, (NSPACE, 16), 0)
    match = (slot < count_v[...]) & (sec_dev == dev)
    picked = jnp.sum(jnp.where(match, code, 0), axis=1, keepdims=True)
    codes[...] = jnp.broadcast_to(picked, (NSPACE, BLOCK))[:, None, :]

    for k in range(NB):
        j = k % GROUP - GROUP // 2
        row = weight[k:k + 1, :].astype(jnp.float32) * (2.0 ** (-j * j * DELTA * DELTA))
        wb[k] = jnp.broadcast_to(row, (16, CH)).astype(jnp.bfloat16)

    pl.semaphore_wait(barrier, NSPACE - 1 + 2)

    def ev(flow, i):
        da, db, (r0, n), sa, sb = EVENTS[i]
        if flow == 0:
            origin, to = place(x + da, z + db, core), place(x + sa, z + sb, core)
        else:
            origin, to = place(x + db, z + da, core), place(x + sb, z + sa, core)
        first_row = (flow * HALF + r0) // BLOCK
        blocks = g.at[pl.ds(origin * PER + first_row, n // BLOCK)]
        src = feat.at[pl.ds(first_row, n // BLOCK)] if da == 0 and db == 0 else blocks
        return remote(src, blocks, gs.at[flow, i], gr.at[flow, i], to)

    def code_copy(i):
        to = lax.rem(me + i, NSPACE)
        return remote(codes.at[to], codes_in.at[me], ks.at[i], kr.at[i], to)

    def to_partner(c):
        blocks = g.at[pl.ds((c * NCORE + core) * PER, PER)]
        return remote(blocks, blocks, ps.at[c], pr.at[c], partner)

    def start(*events):
        for i in events:
            for flow in (0, 1):
                ev(flow, i).start()

    def arrived(*events):
        for i in events:
            for flow in (0, 1):
                ev(flow, i).wait_recv()

    def chip_at(dx, dz):
        return lax.rem(x + dx + NX, NX) * NZ + lax.rem(z + dz + NZ, NZ)

    start(0, 1, 2, 3)
    own_out = remote(feat, g.at[pl.ds(me * PER, PER)], ps.at[NX * NZ], pr.at[NX * NZ], partner)
    own_out.start()

    @pl.loop(1, NSPACE)
    def _(i):
        code_copy(i).start()
    own_code = pltpu.make_async_copy(codes.at[me], codes_in.at[me], ls.at[1])
    own_code.start()

    for a in range(3):
        for b in range(PER):
            at = pl.ds(pl.multiple_of(me * ROWS + b * BLOCK, BLOCK), BLOCK)
            posb[a, b] = jnp.broadcast_to(pos[a:a + 1, at], (BLOCK, BLOCK)).T
        at = pl.ds(pl.multiple_of(core * 512 + (chip // 4) * BLOCK, BLOCK), BLOCK)
        wt[a] = jnp.broadcast_to(wave[a:a + 1, at].astype(jnp.float32), (BLOCK, BLOCK)).T

    @pl.loop(0, NSPACE * PER // 8)
    def _(i):
        for j in range(8):
            at = pl.ds(pl.multiple_of(i * 1024 + j * BLOCK, BLOCK), BLOCK)
            posq[i * 8 + j] = pos[:, at]
    acc[...] = jnp.zeros_like(acc)
    s_acc[...] = jnp.zeros_like(s_acc)

    @pl.loop(0, PER)
    def _(b):
        at = pl.ds(pl.multiple_of(b * BLOCK, BLOCK), BLOCK)
        for h in range(NCORE):
            for part in range(2):
                k0 = h * 512 + part * 256
                t = None
                for a in range(3):
                    n = wave[a:a + 1, k0:k0 + 256].astype(jnp.float32)
                    p = posb[a, b]
                    term = jnp.concatenate([p, p], 1) * n
                    t = term if t is None else t + term
                c, s = cos_sin_turns(t * 0.125)
                col = h * 1024 + part * 256
                cs[at, col:col + 256] = c
                cs[at, col + 512:col + 768] = s

    mine = pl.ds(pl.multiple_of(lax.rem(chip, 4) * 32, 32), 32)
    nrow = [wt[a, mine, :] for a in range(3)]

    def distance(target, source):
        total = None
        there = posq[source]
        for a in range(3):
            off = jnp.abs(there[a:a + 1, :] - posb[a, target])
            off = jnp.minimum(off, 8.0 - off)
            total = off * off if total is None else total + off * off
        return jnp.sqrt(total) * SCALE

    def half_pair(target, source, f32_rows):
        es = expansion(distance(target, source))
        f = f32_rows.astype(jnp.bfloat16).reshape(8, 16, CH)
        total = None
        for k in range(0, NB, 2):
            lhs = jnp.concatenate(es[k:k + 2], 1)
            rhs = jnp.concatenate([(f * wb[k + j][None]).reshape(BLOCK, CH) for j in range(2)], 0)
            part = jnp.dot(lhs, rhs, preferred_element_type=jnp.float32)
            total = part if total is None else total + part
        return total

    def add_rows(targets, values):
        for b in range(PER):
            rows = acc[b * BLOCK:(b + 1) * BLOCK, :]
            for target, value in zip(targets, values):
                rows = rows + jnp.where(target == b, value, 0.0)
            acc[b * BLOCK:(b + 1) * BLOCK, :] = rows

    def add_factors(c):
        at = [pl.ds(pl.multiple_of(c * 1024 + i * BLOCK, BLOCK), BLOCK) for i in range(8)]
        blocks = []
        for i in range(8):
            t = nrow[0] * pos[0:1, at[i]] + nrow[1] * pos[1:2, at[i]] + nrow[2] * pos[2:3, at[i]]
            co, si = cos_sin_turns(t * 0.125)
            blocks.append(jnp.concatenate([co, si], 0))
        rows = g[pl.ds(c * NCORE * PER, NCORE * PER)].reshape(NCORE * ROWS, CH)
        s_acc[...] += jnp.dot(jnp.concatenate(blocks, 1), rows, preferred_element_type=jnp.float32)

    def slot_of(e):
        value = code_s[e, 0, 0]
        v = jnp.maximum(value - 1, 0)
        return value, v // BLOCK, lax.rem(v, BLOCK)

    def own_slot(s):
        f = g[second[s]].astype(jnp.float32)
        return lax.rem(first[s], PER), second[s], jnp.where(s < count[0], f, 0.0)

    def chosen_block(e):
        value, target, source = slot_of(e)
        local = jnp.where(value > 0, source - e * PER, -1)
        f = None
        for b in range(PER):
            block = jnp.where(local == b, g[e * PER + b].astype(jnp.float32), 0.0)
            f = block if f is None else f + block
        return target, source, f

    def loaded_block(e):
        value, target, source = slot_of(e)
        return target, source, jnp.where(value > 0, g[source].astype(jnp.float32), 0.0)

    def add_pairs(items):
        add_rows([t for t, _, _ in items], [half_pair(*item) for item in items])

    def early(*chips):
        add_pairs([chosen_block(c * NCORE + h) for c in chips for h in range(NCORE)])

    def both(c):
        to_partner(c).wait_recv()

    near = ((1, 0), (-1, 0), (0, 1), (0, -1))
    diag = ((1, 1), (1, -1), (-1, 1), (-1, -1))
    far = ((2, 0), (0, 2))
    knight = ((2, 1), (2, -1), (1, 2), (-1, 2))

    def forward(group):
        for dx, dz in group:
            to_partner(chip_at(dx, dz)).start()

    def near_factors(i):
        sign, along = 1 - 2 * lax.rem(i, 2), i // 2
        c = chip_at(sign * (1 - along), sign * along)
        both(c)
        add_factors(c)

    def diag_factors(i):
        c = chip_at(1 - 2 * (i // 2), 1 - 2 * lax.rem(i, 2))
        both(c)
        add_factors(c)

    def two_factors(i):
        late = i // 4
        add_factors(chip_at(2 * (1 - late) + late * ((i - 4) + (i - 4) // 2), (1 - late) * i + 2 * late))

    arrived(0, 1)
    start(4, 5, 6, 7, 8, 9)
    arrived(2, 3)
    start(14, 15)
    forward(near)
    own.wait()
    own_out.wait_recv()
    add_factors(chip)

    @pl.loop(1, NSPACE)
    def _(i):
        code_copy(i).wait_recv()
    own_code.wait()
    to_smem = pltpu.make_async_copy(codes_in, code_s, ls.at[2])
    to_smem.start()
    to_smem.wait()
    pl.loop(0, 4)(near_factors)
    arrived(4, 7)
    start(10, 11, 12, 13)
    early(chip, chip_at(1, 0))
    arrived(5, 6, 8, 9)
    start(16, 17, 18, 19)
    forward(diag)
    arrived(14, 15)
    forward(far)
    early(chip_at(-1, 0), chip_at(0, 1))
    arrived(10, 13)
    start(20, 21)
    pl.loop(0, 4)(diag_factors)
    early(chip_at(0, -1), chip_at(1, 1))
    arrived(11, 12, 16, 17, 18, 19)
    forward(knight)
    early(chip_at(1, -1), chip_at(-1, 1))
    arrived(20, 21)
    forward(((2, 2),))
    for dx, dz in far:
        both(chip_at(dx, dz))
    early(chip_at(2, 0), chip_at(0, 2))
    for dx, dz in knight + ((2, 2),):
        both(chip_at(dx, dz))
    pl.loop(0, 7)(two_factors)

    n = [r[:, 0:1] for r in nrow]
    q = (2.0 * math.pi / 8.0) ** 2 * (n[0] * n[0] + n[1] * n[1] + n[2] * n[2])
    sm = smear[...]
    kern = (4.0 * math.pi / q) * jnp.exp(-0.5 * q * (sm * sm))
    fg[core, 0, chip] = (s_acc[0:32, :] * kern).astype(jnp.bfloat16)
    fg[core, 1, chip] = (s_acc[32:64, :] * kern).astype(jnp.bfloat16)

    def f_copy(i):
        own_f = fg.at[core, :, chip]
        return remote(own_f, own_f, fs.at[i], fr.at[i], lax.rem(me + i, NSPACE))

    @pl.loop(1, NSPACE)
    def _(i):
        f_copy(i).start()

    @pl.loop(0, 6)
    def _(i):
        late, last = i // 3, i // 5
        c = chip_at(2 * (1 - late) + late * (1 + 2 * (i - 3) - 2 * last), (1 - late) * (1 + i) + late * (2 + last))
        add_pairs([loaded_block(c * NCORE), loaded_block(c * NCORE + 1), own_slot(2 * i), own_slot(2 * i + 1)])

    add_pairs([own_slot(s) for s in range(12, 16)])

    @pl.loop(1, NSPACE)
    def _(i):
        f_copy(i).wait_recv()

    def message(h):
        at = pl.ds(h * HALF, HALF)
        recip = jnp.dot(cs[at, :], fg[...].reshape(2 * KV, CH), preferred_element_type=jnp.float32)
        recip = recip * (4.0 / math.sqrt(16384.0 * KV))
        m[yme, at, :] = (0.25 * acc[at, :] + recip).astype(jnp.bfloat16)

    def hop(i, origin, rows, to):
        piece = m.at[origin, rows]
        return pltpu.make_async_remote_copy(
            src_ref=piece, dst_ref=piece, send_sem=ms.at[i], recv_sem=mr.at[i],
            device_id={"chan": to}, device_id_type=MESH)

    lo, hi = pl.ds(0, HALF), pl.ds(HALF, HALF)
    c0, c3 = hop(0, yme, lo, yup), hop(3, yme, lo, ydown)
    c1, c2 = hop(1, yme, hi, ydown), hop(2, yme, hi, yup)
    c4, c5 = hop(4, ydown, lo, yup), hop(5, yup, hi, ydown)
    message(0)
    c0.start()
    c3.start()
    message(1)
    c1.start()
    c2.start()

    def mixed(origin):
        rows = pl.ds(pl.multiple_of(origin * CH, CH), CH)
        return jnp.dot(m[origin], mix[rows, :], preferred_element_type=jnp.float32)

    total = feat[...].reshape(ROWS, CH).astype(jnp.float32) + mixed(yme)
    c0.wait_recv()
    c4.start()
    c1.wait_recv()
    c5.start()
    c2.wait_recv()
    total = total + mixed(ydown)
    c3.wait_recv()
    total = total + mixed(yup)
    c4.wait_recv()
    c5.wait_recv()
    out[...] = (total + mixed(yacross)).astype(jnp.bfloat16)

    for i in range(NEV):
        for flow in (0, 1):
            ev(flow, i).wait_send()
    own_out.wait_send()
    for c in (c0, c1, c2, c3, c4, c5):
        c.wait_send()

    @pl.loop(1, NSPACE)
    def _(i):
        code_copy(i).wait_send()
        f_copy(i).wait_send()

    @pl.loop(1, NX * NZ)
    def _(i):
        to_partner(lax.rem(chip + i, NX * NZ)).wait_send()


def body(features, positions, pair_first, pair_second, pair_counts, wave_index,
         radial_weight, smearing, mix_weight):
    dma = pltpu.SemaphoreType.DMA
    bf16, f32 = jnp.bfloat16, jnp.float32
    return pl.pallas_call(
        kernel,
        out_shape=jax.ShapeDtypeStruct((ROWS, CH), bf16),
        in_specs=[VM, SM, SM, SM] + [VM] * 8,
        out_specs=VM,
        scratch_shapes=[
            pltpu.VMEM((NSPACE * PER, BLOCK, CH), bf16),
            pltpu.VMEM((NSPACE, 1, BLOCK), jnp.int32),
            pltpu.VMEM((NSPACE, 1, BLOCK), jnp.int32),
            pltpu.SMEM((NSPACE, 1, BLOCK), jnp.int32),
            pltpu.VMEM((NCORE, 2, NX * NZ, 32, CH), bf16),
            pltpu.VMEM((ROWS, 2 * KV), bf16),
            pltpu.VMEM((ROWS, CH), f32),
            pltpu.VMEM((3, PER, BLOCK, BLOCK), f32),
            pltpu.VMEM((NSPACE * PER, 3, BLOCK), f32),
            pltpu.VMEM((3, BLOCK, BLOCK), f32),
            pltpu.VMEM((NB, 16, CH), bf16),
            pltpu.VMEM((64, CH), f32),
            pltpu.VMEM((NCHAN, ROWS, CH), bf16),
            dma((2, NEV)), dma((2, NEV)),
            dma((NSPACE,)), dma((NSPACE,)),
            dma((NX * NZ + 1,)), dma((NX * NZ + 1,)),
            dma((NSPACE,)), dma((NSPACE,)),
            dma((6,)), dma((6,)),
            dma((3,)),
        ],
        compiler_params=pltpu.CompilerParams(collective_id=0, has_side_effects=True),
        name="layer",
    )(features.reshape(PER, BLOCK, CH), pair_first, pair_second, pair_counts, pair_first[None, :], pair_second[None, :],
      pair_counts[None, :], positions, wave_index, radial_weight, smearing[None, :], mix_weight)


def solution(mesh):
    placed = (P("space", "chan"), P(), P("space"), P("space"), P("space"), P(),
              P(None, "chan"), P("chan"), P(None, "chan"))
    return jax.shard_map(
        body, mesh=mesh, in_specs=placed, out_specs=P("space", "chan"), check_vma=False
    )
```

```python
import functools
import math

import jax
import jax.numpy as jnp
from jax import lax
from jax.experimental import pallas as pl
from jax.experimental.pallas import tpu as pltpu
from jax.sharding import PartitionSpec as P

BLOCK = 128
NX, NZ, NCORE, NCHAN = 4, 4, 2, 4
NSPACE = NX * NZ * NCORE
ROWS = 512
CH = 128
KV = 1024
NB = 32
MESH = pl.DeviceIdType.MESH
VM = pl.BlockSpec(memory_space=pltpu.VMEM)
SM = pl.BlockSpec(memory_space=pltpu.SMEM)

REACH = 4.0 * math.sqrt(3.0)
STEP = REACH / (NB - 1)
SPREAD = 1.5 * STEP
SCALE = math.sqrt(math.log2(math.e)) / SPREAD
DELTA = STEP * SCALE
GROUP = 8
PER = ROWS // BLOCK

SIN_C = (3.14159264, -5.167710084, 2.550077523, -0.5982912856, 0.0776576603)
COS_C = (0.9999999532, -4.934792831, 4.058411353, -1.331876568, 0.2196896111)


def horner(v, coeffs):
    out = coeffs[-1] * v + coeffs[-2]
    for c in coeffs[-3::-1]:
        out = out * v + c
    return out


def cos_sin_turns(t):
    u = t - jnp.floor(t + 0.5)
    v = u * u
    s = u * horner(v, SIN_C)
    c = horner(v, COS_C)
    s2 = s + s
    return (1.0 - s2 * s).astype(jnp.bfloat16), (s2 * c).astype(jnp.bfloat16)


def remote(src, dst, send, recv, space):
    return pltpu.make_async_remote_copy(
        src_ref=src, dst_ref=dst, send_sem=send, recv_sem=recv,
        device_id={"space": space}, device_id_type=MESH,
    )


def place(x, z, core):
    return (lax.rem(x + 2 * NX, NX) * NZ + lax.rem(z + 2 * NZ, NZ)) * NCORE + core


HALF = ROWS // 2
QUART = ROWS // 4
FULL, LO, HI = (0, HALF), (0, QUART), (QUART, QUART)
EVENTS = (
    (0, 0, FULL, 1, 0), (0, 0, FULL, -1, 0), (0, 0, FULL, 0, 1), (0, 0, FULL, 0, -1),
    (-1, 0, LO, 1, 0), (-1, 0, FULL, 0, 1), (-1, 0, FULL, 0, -1),
    (1, 0, HI, -1, 0), (1, 0, FULL, 0, 1), (1, 0, FULL, 0, -1),
    (-2, 0, LO, 0, 1), (-2, 0, LO, 0, -1), (2, 0, HI, 0, 1), (2, 0, HI, 0, -1),
    (0, -1, LO, 0, 1), (0, 1, HI, 0, -1),
    (-1, -1, LO, 0, 1), (-1, 1, HI, 0, -1), (1, -1, LO, 0, 1), (1, 1, HI, 0, -1),
    (-2, -1, LO, 0, 1), (2, 1, HI, 0, -1),
)
NEV = len(EVENTS)


def expansion(d):
    out = [None] * NB
    half = GROUP // 2
    for c in range(half, NB, GROUP):
        a, b = d - c * DELTA, c * DELTA - d
        mid = jnp.exp2(a * b)
        up, down = jnp.exp2(a * (2.0 * DELTA)), jnp.exp2(b * (2.0 * DELTA))
        out[c] = mid
        e = mid
        for j in range(1, GROUP - half):
            e = e * up
            out[c + j] = e
        e = mid
        for j in range(1, half + 1):
            e = e * down
            out[c - j] = e
    return [e.astype(jnp.bfloat16) for e in out]


def kernel(feat, first, second, count, first_v, second_v, count_v, pos, wave, weight, smear, mix, out,
           g, codes, codes_in, code_s, fg, cs, acc, posb, posq, wt, wb, s_acc, m,
           gs, gr, ks, kr, ps, pr, fs, fr, ms, mr, ls):
    me = lax.axis_index("space")
    yme = lax.axis_index("chan")
    core = lax.rem(me, NCORE)
    chip = me // NCORE
    x, z = chip // NZ, lax.rem(chip, NZ)
    partner = chip * NCORE + (1 - core)
    yup, ydown = lax.rem(yme + 1, NCHAN), lax.rem(yme + NCHAN - 1, NCHAN)
    yacross = lax.rem(yme + 2, NCHAN)

    barrier = pltpu.get_barrier_semaphore()

    @pl.loop(1, NSPACE)
    def _(i):
        pl.semaphore_signal(barrier, inc=1, device_id={"space": lax.rem(me + i, NSPACE)},
                            device_id_type=MESH)
    for peer in (yup, ydown):
        pl.semaphore_signal(barrier, inc=1, device_id={"chan": peer}, device_id_type=MESH)

    own = pltpu.make_async_copy(feat, g.at[pl.ds(me * PER, PER)], ls.at[0])
    own.start()

    sec = second_v[...]
    sec_dev = sec // PER
    code = (sec - sec_dev * PER) * BLOCK + first_v[...] + 1
    slot = lax.broadcasted_iota(jnp.int32, (NSPACE, 16), 1)
    dev = lax.broadcasted_iota(jnp.int32, (NSPACE, 16), 0)
    match = (slot < count_v[...]) & (sec_dev == dev)
    picked = jnp.sum(jnp.where(match, code, 0), axis=1, keepdims=True)
    codes[...] = jnp.broadcast_to(picked, (NSPACE, BLOCK))[:, None, :]

    for k in range(NB):
        j = k % GROUP - GROUP // 2
        row = weight[k:k + 1, :].astype(jnp.float32) * (2.0 ** (-j * j * DELTA * DELTA))
        wb[k] = jnp.broadcast_to(row, (16, CH)).astype(jnp.bfloat16)

    pl.semaphore_wait(barrier, NSPACE - 1 + 2)

    def ev(flow, i):
        da, db, (r0, n), sa, sb = EVENTS[i]
        if flow == 0:
            origin, to = place(x + da, z + db, core), place(x + sa, z + sb, core)
        else:
            origin, to = place(x + db, z + da, core), place(x + sb, z + sa, core)
        first_row = (flow * HALF + r0) // BLOCK
        blocks = g.at[pl.ds(origin * PER + first_row, n // BLOCK)]
        src = feat.at[pl.ds(first_row, n // BLOCK)] if da == 0 and db == 0 else blocks
        return remote(src, blocks, gs.at[flow, i], gr.at[flow, i], to)

    def code_copy(i):
        to = lax.rem(me + i, NSPACE)
        return remote(codes.at[to], codes_in.at[me], ks.at[i], kr.at[i], to)

    def to_partner(c):
        blocks = g.at[pl.ds((c * NCORE + core) * PER, PER)]
        return remote(blocks, blocks, ps.at[c], pr.at[c], partner)

    def start(*events):
        for i in events:
            for flow in (0, 1):
                ev(flow, i).start()

    def arrived(*events):
        for i in events:
            for flow in (0, 1):
                ev(flow, i).wait_recv()

    def chip_at(dx, dz):
        return lax.rem(x + dx + NX, NX) * NZ + lax.rem(z + dz + NZ, NZ)

    start(0, 1, 2, 3)
    own_out = remote(feat, g.at[pl.ds(me * PER, PER)], ps.at[NX * NZ], pr.at[NX * NZ], partner)
    own_out.start()

    @pl.loop(1, NSPACE)
    def _(i):
        code_copy(i).start()
    own_code = pltpu.make_async_copy(codes.at[me], codes_in.at[me], ls.at[1])
    own_code.start()

    for a in range(3):
        for b in range(PER):
            at = pl.ds(pl.multiple_of(me * ROWS + b * BLOCK, BLOCK), BLOCK)
            posb[a, b] = jnp.broadcast_to(pos[a:a + 1, at], (BLOCK, BLOCK)).T
        at = pl.ds(pl.multiple_of(core * 512 + (chip // 4) * BLOCK, BLOCK), BLOCK)
        wt[a] = jnp.broadcast_to(wave[a:a + 1, at].astype(jnp.float32), (BLOCK, BLOCK)).T

    @pl.loop(0, NSPACE * PER // 8)
    def _(i):
        for j in range(8):
            at = pl.ds(pl.multiple_of(i * 1024 + j * BLOCK, BLOCK), BLOCK)
            posq[i * 8 + j] = pos[:, at]
    acc[...] = jnp.zeros_like(acc)
    s_acc[...] = jnp.zeros_like(s_acc)

    @pl.loop(0, PER)
    def _(b):
        at = pl.ds(pl.multiple_of(b * BLOCK, BLOCK), BLOCK)
        for h in range(NCORE):
            for part in range(2):
                k0 = h * 512 + part * 256
                t = None
                for a in range(3):
                    n = wave[a:a + 1, k0:k0 + 256].astype(jnp.float32)
                    p = posb[a, b]
                    term = jnp.concatenate([p, p], 1) * n
                    t = term if t is None else t + term
                c, s = cos_sin_turns(t * 0.125)
                col = h * 1024 + part * 256
                cs[at, col:col + 256] = c
                cs[at, col + 512:col + 768] = s

    mine = pl.ds(pl.multiple_of(lax.rem(chip, 4) * 32, 32), 32)
    nrow = [wt[a, mine, :] for a in range(3)]

    def distance(target, source):
        total = None
        there = posq[source]
        for a in range(3):
            off = jnp.abs(there[a:a + 1, :] - posb[a, target])
            off = jnp.minimum(off, 8.0 - off)
            total = off * off if total is None else total + off * off
        return jnp.sqrt(total) * SCALE

    def half_pair(target, source, f32_rows):
        es = expansion(distance(target, source))
        f = f32_rows.astype(jnp.bfloat16).reshape(8, 16, CH)
        total = None
        for k in range(0, NB, 2):
            lhs = jnp.concatenate(es[k:k + 2], 1)
            rhs = jnp.concatenate([(f * wb[k + j][None]).reshape(BLOCK, CH) for j in range(2)], 0)
            part = jnp.dot(lhs, rhs, preferred_element_type=jnp.float32)
            total = part if total is None else total + part
        return total

    def add_rows(targets, values):
        for b in range(PER):
            rows = acc[b * BLOCK:(b + 1) * BLOCK, :]
            for target, value in zip(targets, values):
                rows = rows + jnp.where(target == b, value, 0.0)
            acc[b * BLOCK:(b + 1) * BLOCK, :] = rows

    def add_factors(c):
        at = [pl.ds(pl.multiple_of(c * 1024 + i * BLOCK, BLOCK), BLOCK) for i in range(8)]
        blocks = []
        for i in range(8):
            t = nrow[0] * pos[0:1, at[i]] + nrow[1] * pos[1:2, at[i]] + nrow[2] * pos[2:3, at[i]]
            co, si = cos_sin_turns(t * 0.125)
            blocks.append(jnp.concatenate([co, si], 0))
        rows = g[pl.ds(c * NCORE * PER, NCORE * PER)].reshape(NCORE * ROWS, CH)
        s_acc[...] += jnp.dot(jnp.concatenate(blocks, 1), rows, preferred_element_type=jnp.float32)

    def slot_of(e):
        value = code_s[e, 0, 0]
        v = jnp.maximum(value - 1, 0)
        return value, v // BLOCK, lax.rem(v, BLOCK)

    def own_slot(s):
        f = g[second[s]].astype(jnp.float32)
        return lax.rem(first[s], PER), second[s], jnp.where(s < count[0], f, 0.0)

    def chosen_block(e):
        value, target, source = slot_of(e)
        local = jnp.where(value > 0, source - e * PER, -1)
        f = None
        for b in range(PER):
            block = jnp.where(local == b, g[e * PER + b].astype(jnp.float32), 0.0)
            f = block if f is None else f + block
        return target, source, f

    def loaded_block(e):
        value, target, source = slot_of(e)
        return target, source, jnp.where(value > 0, g[source].astype(jnp.float32), 0.0)

    def add_pairs(items):
        add_rows([t for t, _, _ in items], [half_pair(*item) for item in items])

    def early(*chips):
        add_pairs([chosen_block(c * NCORE + h) for c in chips for h in range(NCORE)])

    def both(c):
        to_partner(c).wait_recv()

    near = ((1, 0), (-1, 0), (0, 1), (0, -1))
    diag = ((1, 1), (1, -1), (-1, 1), (-1, -1))
    far = ((2, 0), (0, 2))
    knight = ((2, 1), (2, -1), (1, 2), (-1, 2))

    def forward(group):
        for dx, dz in group:
            to_partner(chip_at(dx, dz)).start()

    def near_factors(i):
        sign, along = 1 - 2 * lax.rem(i, 2), i // 2
        c = chip_at(sign * (1 - along), sign * along)
        both(c)
        add_factors(c)

    def diag_factors(i):
        c = chip_at(1 - 2 * (i // 2), 1 - 2 * lax.rem(i, 2))
        both(c)
        add_factors(c)

    def far_factors(i):
        c = chip_at(2 * (1 - i), 2 * i)
        both(c)
        add_factors(c)

    def knight_factors(i):
        sign, along = 1 - 2 * lax.rem(i, 2), i // 2
        c = chip_at(2 * (1 - along) + sign * along, sign * (1 - along) + 2 * along)
        both(c)
        add_factors(c)

    own.wait()
    own_out.wait_recv()
    add_factors(chip)
    arrived(0, 1)
    start(4, 5, 6, 7, 8, 9)
    arrived(2, 3)
    start(14, 15)
    forward(near)

    @pl.loop(1, NSPACE)
    def _(i):
        code_copy(i).wait_recv()
    own_code.wait()
    to_smem = pltpu.make_async_copy(codes_in, code_s, ls.at[2])
    to_smem.start()
    to_smem.wait()
    arrived(4, 7)
    start(10, 11, 12, 13)
    pl.loop(0, 4)(near_factors)
    arrived(5, 6, 8, 9)
    start(16, 17, 18, 19)
    forward(diag)
    arrived(14, 15)
    forward(far)
    early(chip, chip_at(1, 0))
    arrived(10, 13)
    start(20, 21)
    early(chip_at(-1, 0), chip_at(0, 1))
    arrived(11, 12, 16, 17, 18, 19)
    forward(knight)
    pl.loop(0, 4)(diag_factors)
    pl.loop(0, 2)(far_factors)
    early(chip_at(0, -1), chip_at(1, 1))
    arrived(20, 21)
    forward(((2, 2),))
    pl.loop(0, 4)(knight_factors)
    early(chip_at(1, -1), chip_at(-1, 1))
    both(chip_at(2, 2))
    add_factors(chip_at(2, 2))

    n = [r[:, 0:1] for r in nrow]
    q = (2.0 * math.pi / 8.0) ** 2 * (n[0] * n[0] + n[1] * n[1] + n[2] * n[2])
    sm = smear[...]
    kern = (4.0 * math.pi / q) * jnp.exp(-0.5 * q * (sm * sm))
    fg[core, 0, chip] = (s_acc[0:32, :] * kern).astype(jnp.bfloat16)
    fg[core, 1, chip] = (s_acc[32:64, :] * kern).astype(jnp.bfloat16)

    def f_copy(i):
        own_f = fg.at[core, :, chip]
        return remote(own_f, own_f, fs.at[i], fr.at[i], lax.rem(me + i, NSPACE))

    @pl.loop(1, NSPACE)
    def _(i):
        f_copy(i).start()

    @pl.loop(0, 8)
    def _(i):
        late, last = i // 4, i // 7
        dx = 2 * (1 - late) + late * ((i - 4) + (i - 4) // 2 - last)
        c = chip_at(dx, (1 - late) * i + late * (2 + last))
        add_pairs([loaded_block(c * NCORE), loaded_block(c * NCORE + 1), own_slot(2 * i), own_slot(2 * i + 1)])

    @pl.loop(1, NSPACE)
    def _(i):
        f_copy(i).wait_recv()

    def message(b):
        at = pl.ds(b * BLOCK, BLOCK)
        recip = jnp.dot(cs[at, :], fg[...].reshape(2 * KV, CH), preferred_element_type=jnp.float32)
        recip = recip * (4.0 / math.sqrt(16384.0 * KV))
        m[yme, b] = (0.25 * acc[at, :] + recip).astype(jnp.bfloat16)

    def hop(i, origin, b, to):
        piece = m.at[origin, b]
        return pltpu.make_async_remote_copy(
            src_ref=piece, dst_ref=piece, send_sem=ms.at[i], recv_sem=mr.at[i],
            device_id={"chan": to}, device_id_type=MESH)

    ups = [hop(b, yme, b, yup) for b in range(PER)]
    downs = [hop(PER + b, yme, b, ydown) for b in range(PER)]
    relays = [hop(2 * PER + b, ydown, b, yup) for b in (0, 1)] + [hop(2 * PER + b, yup, b, ydown) for b in (2, 3)]
    message(0)
    message(2)
    ups[0].start()
    downs[2].start()
    message(1)
    message(3)
    ups[1].start()
    downs[3].start()
    ups[2].start()
    downs[0].start()
    ups[3].start()
    downs[1].start()

    def mixed(origin):
        rows = pl.ds(pl.multiple_of(origin * CH, CH), CH)
        return jnp.dot(m[origin].reshape(ROWS, CH), mix[rows, :], preferred_element_type=jnp.float32)

    ups[0].wait_recv()
    relays[0].start()
    downs[2].wait_recv()
    relays[2].start()
    ups[1].wait_recv()
    relays[1].start()
    downs[3].wait_recv()
    relays[3].start()
    total = feat[...].reshape(ROWS, CH).astype(jnp.float32) + mixed(yme)
    ups[2].wait_recv()
    ups[3].wait_recv()
    total = total + mixed(ydown)
    downs[0].wait_recv()
    downs[1].wait_recv()
    total = total + mixed(yup)
    for c in relays:
        c.wait_recv()
    out[...] = (total + mixed(yacross)).astype(jnp.bfloat16)

    for i in range(NEV):
        for flow in (0, 1):
            ev(flow, i).wait_send()
    own_out.wait_send()
    for c in ups + downs + relays:
        c.wait_send()

    @pl.loop(1, NSPACE)
    def _(i):
        code_copy(i).wait_send()
        f_copy(i).wait_send()

    @pl.loop(1, NX * NZ)
    def _(i):
        to_partner(lax.rem(chip + i, NX * NZ)).wait_send()


def body(features, positions, pair_first, pair_second, pair_counts, wave_index,
         radial_weight, smearing, mix_weight):
    dma = pltpu.SemaphoreType.DMA
    bf16, f32 = jnp.bfloat16, jnp.float32
    return pl.pallas_call(
        kernel,
        out_shape=jax.ShapeDtypeStruct((ROWS, CH), bf16),
        in_specs=[VM, SM, SM, SM] + [VM] * 8,
        out_specs=VM,
        scratch_shapes=[
            pltpu.VMEM((NSPACE * PER, BLOCK, CH), bf16),
            pltpu.VMEM((NSPACE, 1, BLOCK), jnp.int32),
            pltpu.VMEM((NSPACE, 1, BLOCK), jnp.int32),
            pltpu.SMEM((NSPACE, 1, BLOCK), jnp.int32),
            pltpu.VMEM((NCORE, 2, NX * NZ, 32, CH), bf16),
            pltpu.VMEM((ROWS, 2 * KV), bf16),
            pltpu.VMEM((ROWS, CH), f32),
            pltpu.VMEM((3, PER, BLOCK, BLOCK), f32),
            pltpu.VMEM((NSPACE * PER, 3, BLOCK), f32),
            pltpu.VMEM((3, BLOCK, BLOCK), f32),
            pltpu.VMEM((NB, 16, CH), bf16),
            pltpu.VMEM((64, CH), f32),
            pltpu.VMEM((NCHAN, PER, BLOCK, CH), bf16),
            dma((2, NEV)), dma((2, NEV)),
            dma((NSPACE,)), dma((NSPACE,)),
            dma((NX * NZ + 1,)), dma((NX * NZ + 1,)),
            dma((NSPACE,)), dma((NSPACE,)),
            dma((3 * PER,)), dma((3 * PER,)),
            dma((3,)),
        ],
        compiler_params=pltpu.CompilerParams(collective_id=0, has_side_effects=True),
        name="layer",
    )(features.reshape(PER, BLOCK, CH), pair_first, pair_second, pair_counts, pair_first[None, :], pair_second[None, :],
      pair_counts[None, :], positions, wave_index, radial_weight, smearing[None, :], mix_weight)


def solution(mesh):
    placed = (P("space", "chan"), P(), P("space"), P("space"), P("space"), P(),
              P(None, "chan"), P("chan"), P(None, "chan"))
    return jax.shard_map(
        body, mesh=mesh, in_specs=placed, out_specs=P("space", "chan"), check_vma=False
    )
```

```python
import functools
import math

import jax
import jax.numpy as jnp
from jax import lax
from jax.experimental import pallas as pl
from jax.experimental.pallas import tpu as pltpu
from jax.sharding import PartitionSpec as P

BLOCK = 128
NX, NZ, NCORE, NCHAN = 4, 4, 2, 4
NSPACE = NX * NZ * NCORE
ROWS = 512
CH = 128
KV = 1024
NB = 32
MESH = pl.DeviceIdType.MESH
VM = pl.BlockSpec(memory_space=pltpu.VMEM)
SM = pl.BlockSpec(memory_space=pltpu.SMEM)

REACH = 4.0 * math.sqrt(3.0)
STEP = REACH / (NB - 1)
SPREAD = 1.5 * STEP
SCALE = math.sqrt(math.log2(math.e)) / SPREAD
DELTA = STEP * SCALE
GROUP = 8
PER = ROWS // BLOCK

SIN_C = (3.14159264, -5.167710084, 2.550077523, -0.5982912856, 0.0776576603)
COS_C = (0.9999999532, -4.934792831, 4.058411353, -1.331876568, 0.2196896111)


def horner(v, coeffs):
    out = coeffs[-1] * v + coeffs[-2]
    for c in coeffs[-3::-1]:
        out = out * v + c
    return out


def cos_sin_turns(t):
    u = t - jnp.floor(t + 0.5)
    v = u * u
    s = u * horner(v, SIN_C)
    c = horner(v, COS_C)
    s2 = s + s
    return (1.0 - s2 * s).astype(jnp.bfloat16), (s2 * c).astype(jnp.bfloat16)


def remote(src, dst, send, recv, space):
    return pltpu.make_async_remote_copy(
        src_ref=src, dst_ref=dst, send_sem=send, recv_sem=recv,
        device_id={"space": space}, device_id_type=MESH,
    )


def place(x, z, core):
    return (lax.rem(x + 2 * NX, NX) * NZ + lax.rem(z + 2 * NZ, NZ)) * NCORE + core


HALF = ROWS // 2
QUART = ROWS // 4
FULL, LO, HI = (0, HALF), (0, QUART), (QUART, QUART)
EVENTS = (
    (0, 0, FULL, 1, 0), (0, 0, FULL, -1, 0), (0, 0, FULL, 0, 1), (0, 0, FULL, 0, -1),
    (-1, 0, LO, 1, 0), (-1, 0, FULL, 0, 1), (-1, 0, FULL, 0, -1),
    (1, 0, HI, -1, 0), (1, 0, FULL, 0, 1), (1, 0, FULL, 0, -1),
    (-2, 0, LO, 0, 1), (-2, 0, LO, 0, -1), (2, 0, HI, 0, 1), (2, 0, HI, 0, -1),
    (0, -1, LO, 0, 1), (0, 1, HI, 0, -1),
    (-1, -1, LO, 0, 1), (-1, 1, HI, 0, -1), (1, -1, LO, 0, 1), (1, 1, HI, 0, -1),
    (-2, -1, LO, 0, 1), (2, 1, HI, 0, -1),
)
NEV = len(EVENTS)


def expansion(d2):
    out = [None] * NB
    half = GROUP // 2
    shrink = 1.0 / (4.0 * DELTA * DELTA)
    dk = d2 * shrink
    for c in range(half, NB, GROUP):
        centre = 2.0 * c * DELTA * DELTA
        a = d2 - centre
        mid = jnp.exp2(a * (centre * shrink - dk))
        up, down = jnp.exp2(a), jnp.exp2(centre - d2)
        out[c] = mid
        e = mid
        for j in range(1, GROUP - half):
            e = e * up
            out[c + j] = e
        e = mid
        for j in range(1, half + 1):
            e = e * down
            out[c - j] = e
    return [e.astype(jnp.bfloat16) for e in out]


def kernel(feat, first, second, count, first_v, second_v, count_v, pos, wave, weight, smear, mix, out,
           g, table, codes, code_s, fg, cs, acc, posb, posq, wt, wb, s_acc, m,
           gs, gr, ks, kr, ps, pr, fs, fr, ms, mr, ls):
    me = lax.axis_index("space")
    yme = lax.axis_index("chan")
    core = lax.rem(me, NCORE)
    chip = me // NCORE
    x, z = chip // NZ, lax.rem(chip, NZ)
    partner = chip * NCORE + (1 - core)
    yup, ydown = lax.rem(yme + 1, NCHAN), lax.rem(yme + NCHAN - 1, NCHAN)
    yacross = lax.rem(yme + 2, NCHAN)

    barrier = pltpu.get_barrier_semaphore()

    xpeers = [place(x + i, z, core) for i in (1, 2, 3)]
    zpeers = [place(x, z + i, core) for i in (1, 2, 3)]
    for peer in xpeers + zpeers + [partner]:
        pl.semaphore_signal(barrier, inc=1, device_id={"space": peer}, device_id_type=MESH)
    for peer in (yup, ydown):
        pl.semaphore_signal(barrier, inc=1, device_id={"chan": peer}, device_id_type=MESH)

    own = pltpu.make_async_copy(feat, g.at[pl.ds(me * PER, PER)], ls.at[0])
    own.start()

    slot = lax.broadcasted_iota(jnp.int32, (1, 16), 1)
    listed = jnp.where(slot < count_v[...], first_v[...] + BLOCK * second_v[...] + 1, 0)
    table[core, x, z] = jnp.zeros((1, BLOCK), jnp.int32)
    table[core, x, z, :, 0:16] = listed

    for k in range(NB):
        j = k % GROUP - GROUP // 2
        row = weight[k:k + 1, :].astype(jnp.float32) * (2.0 ** (-j * j * DELTA * DELTA))
        wb[k] = jnp.broadcast_to(row, (16, CH)).astype(jnp.bfloat16)

    pl.semaphore_wait(barrier, 9)

    def ev(flow, i):
        da, db, (r0, n), sa, sb = EVENTS[i]
        if flow == 0:
            origin, to = place(x + da, z + db, core), place(x + sa, z + sb, core)
        else:
            origin, to = place(x + db, z + da, core), place(x + sb, z + sa, core)
        first_row = (flow * HALF + r0) // BLOCK
        blocks = g.at[pl.ds(origin * PER + first_row, n // BLOCK)]
        src = feat.at[pl.ds(first_row, n // BLOCK)] if da == 0 and db == 0 else blocks
        return remote(src, blocks, gs.at[flow, i], gr.at[flow, i], to)

    def table_x(i):
        mine = table.at[core, x, z]
        return remote(mine, mine, ks.at[i], kr.at[i], xpeers[i])

    def table_z(i):
        mine = table.at[core, :, z]
        return remote(mine, mine, ks.at[3 + i], kr.at[3 + i], zpeers[i])

    table_core = remote(table.at[core], table.at[core], ks.at[6], kr.at[6], partner)

    def to_partner(c):
        blocks = g.at[pl.ds((c * NCORE + core) * PER, PER)]
        return remote(blocks, blocks, ps.at[c], pr.at[c], partner)

    def start(*events):
        for i in events:
            for flow in (0, 1):
                ev(flow, i).start()

    def arrived(*events):
        for i in events:
            for flow in (0, 1):
                ev(flow, i).wait_recv()

    def chip_at(dx, dz):
        return lax.rem(x + dx + NX, NX) * NZ + lax.rem(z + dz + NZ, NZ)

    start(0, 1, 2, 3)
    own_out = remote(feat, g.at[pl.ds(me * PER, PER)], ps.at[NX * NZ], pr.at[NX * NZ], partner)
    own_out.start()

    for i in range(3):
        table_x(i).start()

    for a in range(3):
        for b in range(PER):
            at = pl.ds(pl.multiple_of(me * ROWS + b * BLOCK, BLOCK), BLOCK)
            posb[a, b] = jnp.broadcast_to(pos[a:a + 1, at], (BLOCK, BLOCK)).T
        at = pl.ds(pl.multiple_of(core * 512 + (chip // 4) * BLOCK, BLOCK), BLOCK)
        wt[a] = jnp.broadcast_to(wave[a:a + 1, at].astype(jnp.float32), (BLOCK, BLOCK)).T

    for i in range(3):
        table_x(i).wait_recv()
    for i in range(3):
        table_z(i).start()

    @pl.loop(0, NSPACE * PER // 8)
    def _(i):
        for j in range(8):
            at = pl.ds(pl.multiple_of(i * 1024 + j * BLOCK, BLOCK), BLOCK)
            posq[i * 8 + j] = pos[:, at]
    acc[...] = jnp.zeros_like(acc)
    s_acc[...] = jnp.zeros_like(s_acc)

    @pl.loop(0, PER)
    def _(b):
        at = pl.ds(pl.multiple_of(b * BLOCK, BLOCK), BLOCK)
        for h in range(NCORE):
            for part in range(2):
                k0 = h * 512 + part * 256
                t = None
                for a in range(3):
                    n = wave[a:a + 1, k0:k0 + 256].astype(jnp.float32)
                    p = posb[a, b]
                    term = jnp.concatenate([p, p], 1) * n
                    t = term if t is None else t + term
                c, s = cos_sin_turns(t * 0.125)
                col = h * 1024 + part * 256
                cs[at, col:col + 256] = c
                cs[at, col + 512:col + 768] = s

    mine = pl.ds(pl.multiple_of(lax.rem(chip, 4) * 32, 32), 32)
    nrow = [wt[a, mine, :] for a in range(3)]

    def distance(target, source):
        total = None
        there = posq[source]
        for a in range(3):
            off = jnp.abs(there[a:a + 1, :] - posb[a, target])
            off = jnp.minimum(off, 8.0 - off)
            total = off * off if total is None else total + off * off
        return jnp.sqrt(total) * (SCALE * 2.0 * DELTA)

    def half_pair(target, source, f32_rows):
        es = expansion(distance(target, source))
        f = f32_rows.astype(jnp.bfloat16).reshape(8, 16, CH)
        total = None
        for k in range(0, NB, 2):
            lhs = jnp.concatenate(es[k:k + 2], 1)
            rhs = jnp.concatenate([(f * wb[k + j][None]).reshape(BLOCK, CH) for j in range(2)], 0)
            part = jnp.dot(lhs, rhs, preferred_element_type=jnp.float32)
            total = part if total is None else total + part
        return total

    def add_rows(targets, values):
        for b in range(PER):
            rows = acc[b * BLOCK:(b + 1) * BLOCK, :]
            for target, value in zip(targets, values):
                rows = rows + jnp.where(target == b, value, 0.0)
            acc[b * BLOCK:(b + 1) * BLOCK, :] = rows

    def add_factors(c):
        at = [pl.ds(pl.multiple_of(c * 1024 + i * BLOCK, BLOCK), BLOCK) for i in range(8)]
        blocks = []
        for i in range(8):
            t = nrow[0] * pos[0:1, at[i]] + nrow[1] * pos[1:2, at[i]] + nrow[2] * pos[2:3, at[i]]
            co, si = cos_sin_turns(t * 0.125)
            blocks.append(jnp.concatenate([co, si], 0))
        rows = g[pl.ds(c * NCORE * PER, NCORE * PER)].reshape(NCORE * ROWS, CH)
        s_acc[...] += jnp.dot(jnp.concatenate(blocks, 1), rows, preferred_element_type=jnp.float32)

    def slot_of(e):
        value = code_s[lax.rem(e, NCORE) * (NX * NZ) + e // NCORE, 0, 0]
        v = jnp.maximum(value - 1, 0)
        return value, v // BLOCK, lax.rem(v, BLOCK)

    def own_slot(s):
        f = g[second[s]].astype(jnp.float32)
        return lax.rem(first[s], PER), second[s], jnp.where(s < count[0], f, 0.0)

    def chosen_block(e):
        value, target, source = slot_of(e)
        local = jnp.where(value > 0, source - e * PER, -1)
        f = None
        for b in range(PER):
            block = jnp.where(local == b, g[e * PER + b].astype(jnp.float32), 0.0)
            f = block if f is None else f + block
        return target, source, f

    def loaded_block(e):
        value, target, source = slot_of(e)
        return target, source, jnp.where(value > 0, g[source].astype(jnp.float32), 0.0)

    def add_pairs(items):
        add_rows([t for t, _, _ in items], [half_pair(*item) for item in items])

    def early(*chips):
        add_pairs([chosen_block(c * NCORE + h) for c in chips for h in range(NCORE)])

    def both(c):
        to_partner(c).wait_recv()

    near = ((1, 0), (-1, 0), (0, 1), (0, -1))
    diag = ((1, 1), (1, -1), (-1, 1), (-1, -1))
    far = ((2, 0), (0, 2))
    knight = ((2, 1), (2, -1), (1, 2), (-1, 2))

    def forward(group):
        for dx, dz in group:
            to_partner(chip_at(dx, dz)).start()

    def near_factors(i):
        sign, along = 1 - 2 * lax.rem(i, 2), i // 2
        c = chip_at(sign * (1 - along), sign * along)
        both(c)
        add_factors(c)

    def diag_factors(i):
        c = chip_at(1 - 2 * (i // 2), 1 - 2 * lax.rem(i, 2))
        both(c)
        add_factors(c)

    def far_factors(i):
        c = chip_at(2 * (1 - i), 2 * i)
        both(c)
        add_factors(c)

    def knight_factors(i):
        sign, along = 1 - 2 * lax.rem(i, 2), i // 2
        c = chip_at(2 * (1 - along) + sign * along, sign * (1 - along) + 2 * along)
        both(c)
        add_factors(c)

    for i in range(3):
        table_z(i).wait_recv()
    table_core.start()
    own.wait()
    own_out.wait_recv()
    add_factors(chip)
    arrived(0, 1)
    start(4, 5, 6, 7, 8, 9)
    arrived(2, 3)
    start(14, 15)
    forward(near)

    table_core.wait_recv()
    rows = table[...].reshape(NSPACE, 1, BLOCK) - me * (PER * BLOCK)
    hit = jnp.where((rows > 0) & (rows <= PER * BLOCK), rows, 0)
    codes[...] = jnp.broadcast_to(jnp.sum(hit, axis=2, keepdims=True), (NSPACE, 1, BLOCK))
    to_smem = pltpu.make_async_copy(codes, code_s, ls.at[2])
    to_smem.start()
    to_smem.wait()
    arrived(4, 7)
    start(10, 11, 12, 13)
    pl.loop(0, 4)(near_factors)
    arrived(5, 6, 8, 9)
    start(16, 17, 18, 19)
    forward(diag)
    arrived(14, 15)
    forward(far)
    early(chip, chip_at(1, 0))
    arrived(10, 13)
    start(20, 21)
    early(chip_at(-1, 0), chip_at(0, 1))
    arrived(11, 12, 16, 17, 18, 19)
    forward(knight)
    pl.loop(0, 4)(diag_factors)
    pl.loop(0, 2)(far_factors)
    early(chip_at(0, -1), chip_at(1, 1))
    arrived(20, 21)
    forward(((2, 2),))
    pl.loop(0, 4)(knight_factors)
    early(chip_at(1, -1), chip_at(-1, 1))
    early(chip_at(2, 0), chip_at(0, 2))
    both(chip_at(2, 2))
    add_factors(chip_at(2, 2))

    n = [r[:, 0:1] for r in nrow]
    q = (2.0 * math.pi / 8.0) ** 2 * (n[0] * n[0] + n[1] * n[1] + n[2] * n[2])
    sm = smear[...]
    kern = (4.0 * math.pi / q) * jnp.exp(-0.5 * q * (sm * sm))
    fg[core, 0, x, z] = (s_acc[0:32, :] * kern).astype(jnp.bfloat16)
    fg[core, 1, x, z] = (s_acc[32:64, :] * kern).astype(jnp.bfloat16)

    def f_x(i):
        mine = fg.at[core, :, x, z]
        return remote(mine, mine, fs.at[i], fr.at[i], xpeers[i])

    def f_z(i):
        mine = fg.at[core, :, :, z]
        return remote(mine, mine, fs.at[3 + i], fr.at[3 + i], zpeers[i])

    f_core = remote(fg.at[core], fg.at[core], fs.at[6], fr.at[6], partner)
    for i in range(3):
        f_x(i).start()

    def late_step(i):
        late, last = i // 3, i // 5
        c = chip_at(2 * (1 - late) + late * (1 + 2 * (i - 3) - 2 * last), (1 - late) * (1 + i) + late * (2 + last))
        add_pairs([loaded_block(c * NCORE), loaded_block(c * NCORE + 1), own_slot(2 * i), own_slot(2 * i + 1)])

    pl.loop(0, 2)(late_step)
    for i in range(3):
        f_x(i).wait_recv()
    for i in range(3):
        f_z(i).start()
    pl.loop(2, 5)(late_step)
    for i in range(3):
        f_z(i).wait_recv()
    f_core.start()
    late_step(5)
    add_pairs([own_slot(s) for s in range(12, 16)])
    f_core.wait_recv()

    def message(b):
        at = pl.ds(b * BLOCK, BLOCK)
        recip = jnp.dot(cs[at, :], fg[...].reshape(2 * KV, CH), preferred_element_type=jnp.float32)
        recip = recip * (4.0 / math.sqrt(16384.0 * KV))
        m[yme, b] = (0.25 * acc[at, :] + recip).astype(jnp.bfloat16)

    def hop(i, origin, b, to):
        piece = m.at[origin, b]
        return pltpu.make_async_remote_copy(
            src_ref=piece, dst_ref=piece, send_sem=ms.at[i], recv_sem=mr.at[i],
            device_id={"chan": to}, device_id_type=MESH)

    ups = [hop(b, yme, b, yup) for b in range(PER)]
    downs = [hop(PER + b, yme, b, ydown) for b in range(PER)]
    relays = [hop(2 * PER + b, ydown, b, yup) for b in (0, 1)] + [hop(2 * PER + b, yup, b, ydown) for b in (2, 3)]
    message(0)
    message(2)
    ups[0].start()
    downs[2].start()
    message(1)
    message(3)
    ups[1].start()
    downs[3].start()
    ups[2].start()
    downs[0].start()
    ups[3].start()
    downs[1].start()

    def mixed(origin):
        rows = pl.ds(pl.multiple_of(origin * CH, CH), CH)
        return jnp.dot(m[origin].reshape(ROWS, CH), mix[rows, :], preferred_element_type=jnp.float32)

    ups[0].wait_recv()
    relays[0].start()
    downs[2].wait_recv()
    relays[2].start()
    ups[1].wait_recv()
    relays[1].start()
    downs[3].wait_recv()
    relays[3].start()
    total = feat[...].reshape(ROWS, CH).astype(jnp.float32) + mixed(yme)
    ups[2].wait_recv()
    ups[3].wait_recv()
    total = total + mixed(ydown)
    downs[0].wait_recv()
    downs[1].wait_recv()
    total = total + mixed(yup)
    for c in relays:
        c.wait_recv()
    out[...] = (total + mixed(yacross)).astype(jnp.bfloat16)

    for i in range(NEV):
        for flow in (0, 1):
            ev(flow, i).wait_send()
    own_out.wait_send()
    for c in ups + downs + relays:
        c.wait_send()

    for i in range(3):
        for c in (table_x(i), table_z(i), f_x(i), f_z(i)):
            c.wait_send()
    table_core.wait_send()
    f_core.wait_send()

    @pl.loop(1, NX * NZ)
    def _(i):
        to_partner(lax.rem(chip + i, NX * NZ)).wait_send()


def body(features, positions, pair_first, pair_second, pair_counts, wave_index,
         radial_weight, smearing, mix_weight):
    dma = pltpu.SemaphoreType.DMA
    bf16, f32 = jnp.bfloat16, jnp.float32
    return pl.pallas_call(
        kernel,
        out_shape=jax.ShapeDtypeStruct((ROWS, CH), bf16),
        in_specs=[VM, SM, SM, SM] + [VM] * 8,
        out_specs=VM,
        scratch_shapes=[
            pltpu.VMEM((NSPACE * PER, BLOCK, CH), bf16),
            pltpu.VMEM((NCORE, NX, NZ, 1, BLOCK), jnp.int32),
            pltpu.VMEM((NSPACE, 1, BLOCK), jnp.int32),
            pltpu.SMEM((NSPACE, 1, BLOCK), jnp.int32),
            pltpu.VMEM((NCORE, 2, NX, NZ, 32, CH), bf16),
            pltpu.VMEM((ROWS, 2 * KV), bf16),
            pltpu.VMEM((ROWS, CH), f32),
            pltpu.VMEM((3, PER, BLOCK, BLOCK), f32),
            pltpu.VMEM((NSPACE * PER, 3, BLOCK), f32),
            pltpu.VMEM((3, BLOCK, BLOCK), f32),
            pltpu.VMEM((NB, 16, CH), bf16),
            pltpu.VMEM((64, CH), f32),
            pltpu.VMEM((NCHAN, PER, BLOCK, CH), bf16),
            dma((2, NEV)), dma((2, NEV)),
            dma((7,)), dma((7,)),
            dma((NX * NZ + 1,)), dma((NX * NZ + 1,)),
            dma((7,)), dma((7,)),
            dma((3 * PER,)), dma((3 * PER,)),
            dma((3,)),
        ],
        compiler_params=pltpu.CompilerParams(collective_id=0, has_side_effects=True),
        name="layer",
    )(features.reshape(PER, BLOCK, CH), pair_first, pair_second, pair_counts, pair_first[None, :], pair_second[None, :],
      pair_counts[None, :], positions, wave_index, radial_weight, smearing[None, :], mix_weight)


def solution(mesh):
    placed = (P("space", "chan"), P(), P("space"), P("space"), P("space"), P(),
              P(None, "chan"), P("chan"), P(None, "chan"))
    return jax.shard_map(
        body, mesh=mesh, in_specs=placed, out_specs=P("space", "chan"), check_vma=False
    )
```

```python
import functools
import math

import jax
import jax.numpy as jnp
from jax import lax
from jax.experimental import pallas as pl
from jax.experimental.pallas import tpu as pltpu
from jax.sharding import PartitionSpec as P

BLOCK = 128
NX, NZ, NCORE, NCHAN = 4, 4, 2, 4
NSPACE = NX * NZ * NCORE
ROWS = 512
CH = 128
KV = 1024
NB = 32
MESH = pl.DeviceIdType.MESH
VM = pl.BlockSpec(memory_space=pltpu.VMEM)
SM = pl.BlockSpec(memory_space=pltpu.SMEM)

REACH = 4.0 * math.sqrt(3.0)
STEP = REACH / (NB - 1)
SPREAD = 1.5 * STEP
SCALE = math.sqrt(math.log2(math.e)) / SPREAD
DELTA = STEP * SCALE
GROUP = 8
PER = ROWS // BLOCK

SIN_C = (3.14159264, -5.167710084, 2.550077523, -0.5982912856, 0.0776576603)
COS_C = (0.9999999532, -4.934792831, 4.058411353, -1.331876568, 0.2196896111)


def horner(v, coeffs):
    out = coeffs[-1] * v + coeffs[-2]
    for c in coeffs[-3::-1]:
        out = out * v + c
    return out


def cos_sin_turns(t):
    u = t - jnp.floor(t + 0.5)
    v = u * u
    s = u * horner(v, SIN_C)
    c = horner(v, COS_C)
    s2 = s + s
    return (1.0 - s2 * s).astype(jnp.bfloat16), (s2 * c).astype(jnp.bfloat16)


def remote(src, dst, send, recv, space):
    return pltpu.make_async_remote_copy(
        src_ref=src, dst_ref=dst, send_sem=send, recv_sem=recv,
        device_id={"space": space}, device_id_type=MESH,
    )


def place(x, z, core):
    return (lax.rem(x + 2 * NX, NX) * NZ + lax.rem(z + 2 * NZ, NZ)) * NCORE + core


HALF = ROWS // 2
QUART = ROWS // 4
FULL, LO, HI = (0, HALF), (0, QUART), (QUART, QUART)
EVENTS = (
    (0, 0, FULL, 1, 0), (0, 0, FULL, -1, 0), (0, 0, FULL, 0, 1), (0, 0, FULL, 0, -1),
    (-1, 0, LO, 1, 0), (-1, 0, FULL, 0, 1), (-1, 0, FULL, 0, -1),
    (1, 0, HI, -1, 0), (1, 0, FULL, 0, 1), (1, 0, FULL, 0, -1),
    (-2, 0, LO, 0, 1), (-2, 0, LO, 0, -1), (2, 0, HI, 0, 1), (2, 0, HI, 0, -1),
    (0, -1, LO, 0, 1), (0, 1, HI, 0, -1),
    (-1, -1, LO, 0, 1), (-1, 1, HI, 0, -1), (1, -1, LO, 0, 1), (1, 1, HI, 0, -1),
    (-2, -1, LO, 0, 1), (2, 1, HI, 0, -1),
)
NEV = len(EVENTS)


def expansion(d2):
    out = [None] * NB
    half = GROUP // 2
    shrink = 1.0 / (4.0 * DELTA * DELTA)
    dk = d2 * shrink
    for c in range(half, NB, GROUP):
        centre = 2.0 * c * DELTA * DELTA
        a = d2 - centre
        mid = jnp.exp2(a * (centre * shrink - dk))
        up, down = jnp.exp2(a), jnp.exp2(centre - d2)
        out[c] = mid
        for sign, ratio, length in ((1, up, GROUP - half - 1), (-1, down, half)):
            e = mid
            for j in range(1, length + 1):
                if j == 3:
                    e, ratio = out[c + 2 * sign], ratio.astype(jnp.bfloat16)
                e = e * ratio
                out[c + sign * j] = e.astype(jnp.bfloat16)
        out[c] = mid.astype(jnp.bfloat16)
    return out


def kernel(feat, first, second, count, first_v, second_v, count_v, pos, wave, weight, smear, mix, out,
           g, table, codes, code_s, fg, cs, acc, posb, posq, wt, wb, s_acc, m,
           gs, gr, ks, kr, ps, pr, fs, fr, ms, mr, ls):
    me = lax.axis_index("space")
    yme = lax.axis_index("chan")
    core = lax.rem(me, NCORE)
    chip = me // NCORE
    x, z = chip // NZ, lax.rem(chip, NZ)
    partner = chip * NCORE + (1 - core)
    yup, ydown = lax.rem(yme + 1, NCHAN), lax.rem(yme + NCHAN - 1, NCHAN)
    yacross = lax.rem(yme + 2, NCHAN)

    barrier = pltpu.get_barrier_semaphore()

    xpeers = [place(x + i, z, core) for i in (1, 2, 3)]
    zpeers = [place(x, z + i, core) for i in (1, 2, 3)]
    for peer in xpeers + zpeers + [partner]:
        pl.semaphore_signal(barrier, inc=1, device_id={"space": peer}, device_id_type=MESH)
    for peer in (yup, ydown):
        pl.semaphore_signal(barrier, inc=1, device_id={"chan": peer}, device_id_type=MESH)

    own = pltpu.make_async_copy(feat, g.at[pl.ds(me * PER, PER)], ls.at[0])
    own.start()

    slot = lax.broadcasted_iota(jnp.int32, (1, 16), 1)
    listed = jnp.where(slot < count_v[...], first_v[...] + BLOCK * second_v[...] + 1, 0)
    table[core, x, z] = jnp.zeros((1, BLOCK), jnp.int32)
    table[core, x, z, :, 0:16] = listed

    for k in range(NB):
        j = k % GROUP - GROUP // 2
        row = weight[k:k + 1, :].astype(jnp.float32) * (2.0 ** (-j * j * DELTA * DELTA))
        wb[k] = jnp.broadcast_to(row, (16, CH)).astype(jnp.bfloat16)

    pl.semaphore_wait(barrier, 9)

    def ev(flow, i):
        da, db, (r0, n), sa, sb = EVENTS[i]
        if flow == 0:
            origin, to = place(x + da, z + db, core), place(x + sa, z + sb, core)
        else:
            origin, to = place(x + db, z + da, core), place(x + sb, z + sa, core)
        first_row = (flow * HALF + r0) // BLOCK
        blocks = g.at[pl.ds(origin * PER + first_row, n // BLOCK)]
        src = feat.at[pl.ds(first_row, n // BLOCK)] if da == 0 and db == 0 else blocks
        return remote(src, blocks, gs.at[flow, i], gr.at[flow, i], to)

    def table_x(i):
        mine = table.at[core, x, z]
        return remote(mine, mine, ks.at[i], kr.at[i], xpeers[i])

    def table_z(i):
        mine = table.at[core, :, z]
        return remote(mine, mine, ks.at[3 + i], kr.at[3 + i], zpeers[i])

    table_core = remote(table.at[core], table.at[core], ks.at[6], kr.at[6], partner)

    def to_partner(c):
        blocks = g.at[pl.ds((c * NCORE + core) * PER, PER)]
        return remote(blocks, blocks, ps.at[c], pr.at[c], partner)

    def start(*events):
        for i in events:
            for flow in (0, 1):
                ev(flow, i).start()

    def arrived(*events):
        for i in events:
            for flow in (0, 1):
                ev(flow, i).wait_recv()

    def chip_at(dx, dz):
        return lax.rem(x + dx + NX, NX) * NZ + lax.rem(z + dz + NZ, NZ)

    for i in range(3):
        table_x(i).start()
    start(0, 1, 2, 3)
    own_out = remote(feat, g.at[pl.ds(me * PER, PER)], ps.at[NX * NZ], pr.at[NX * NZ], partner)
    own_out.start()

    for a in range(3):
        for b in range(PER):
            at = pl.ds(pl.multiple_of(me * ROWS + b * BLOCK, BLOCK), BLOCK)
            posb[a, b] = jnp.broadcast_to(pos[a:a + 1, at], (BLOCK, BLOCK)).T
        at = pl.ds(pl.multiple_of(core * 512 + (chip // 4) * BLOCK, BLOCK), BLOCK)
        wt[a] = jnp.broadcast_to(wave[a:a + 1, at].astype(jnp.float32), (BLOCK, BLOCK)).T

    @pl.loop(0, NSPACE * PER // 8)
    def _(i):
        for j in range(8):
            at = pl.ds(pl.multiple_of(i * 1024 + j * BLOCK, BLOCK), BLOCK)
            posq[i * 8 + j] = pos[:, at]
    acc[...] = jnp.zeros_like(acc)
    s_acc[...] = jnp.zeros_like(s_acc)

    @pl.loop(0, PER)
    def _(b):
        at = pl.ds(pl.multiple_of(b * BLOCK, BLOCK), BLOCK)
        for h in range(NCORE):
            for part in range(2):
                k0 = h * 512 + part * 256
                t = None
                for a in range(3):
                    n = wave[a:a + 1, k0:k0 + 256].astype(jnp.float32)
                    p = posb[a, b]
                    term = jnp.concatenate([p, p], 1) * n
                    t = term if t is None else t + term
                c, s = cos_sin_turns(t * 0.125)
                col = h * 1024 + part * 256
                cs[at, col:col + 256] = c
                cs[at, col + 512:col + 768] = s

    mine = pl.ds(pl.multiple_of(lax.rem(chip, 4) * 32, 32), 32)
    nrow = [wt[a, mine, :] for a in range(3)]

    def distance(target, source):
        total = None
        there = posq[source]
        for a in range(3):
            off = jnp.abs(there[a:a + 1, :] - posb[a, target])
            off = jnp.minimum(off, 8.0 - off)
            total = off * off if total is None else total + off * off
        return jnp.sqrt(total) * (SCALE * 2.0 * DELTA)

    def half_pair(target, source, f32_rows):
        es = expansion(distance(target, source))
        f = f32_rows.astype(jnp.bfloat16).reshape(8, 16, CH)
        total = None
        for k in range(0, NB, 2):
            lhs = jnp.concatenate(es[k:k + 2], 1)
            rhs = jnp.concatenate([(f * wb[k + j][None]).reshape(BLOCK, CH) for j in range(2)], 0)
            part = jnp.dot(lhs, rhs, preferred_element_type=jnp.float32)
            total = part if total is None else total + part
        return total

    def add_rows(targets, values):
        for b in range(PER):
            rows = acc[b * BLOCK:(b + 1) * BLOCK, :]
            for target, value in zip(targets, values):
                rows = rows + jnp.where(target == b, value, 0.0)
            acc[b * BLOCK:(b + 1) * BLOCK, :] = rows

    def add_factors(c):
        at = [pl.ds(pl.multiple_of(c * 1024 + i * BLOCK, BLOCK), BLOCK) for i in range(8)]
        blocks = []
        for i in range(8):
            t = nrow[0] * pos[0:1, at[i]] + nrow[1] * pos[1:2, at[i]] + nrow[2] * pos[2:3, at[i]]
            co, si = cos_sin_turns(t * 0.125)
            blocks.append(jnp.concatenate([co, si], 0))
        rows = g[pl.ds(c * NCORE * PER, NCORE * PER)].reshape(NCORE * ROWS, CH)
        s_acc[...] += jnp.dot(jnp.concatenate(blocks, 1), rows, preferred_element_type=jnp.float32)

    def slot_of(e):
        value = code_s[lax.rem(e, NCORE) * (NX * NZ) + e // NCORE, 0, 0]
        v = jnp.maximum(value - 1, 0)
        return value, v // BLOCK, lax.rem(v, BLOCK)

    def own_slot(s):
        f = g[second[s]].astype(jnp.float32)
        return lax.rem(first[s], PER), second[s], jnp.where(s < count[0], f, 0.0)

    def chosen_block(e):
        value, target, source = slot_of(e)
        local = jnp.where(value > 0, source - e * PER, -1)
        f = jnp.zeros((BLOCK, CH), jnp.bfloat16)
        for b in range(PER):
            f = jnp.where(local == b, g[e * PER + b], f)
        return target, source, f.astype(jnp.float32)

    def loaded_block(e):
        value, target, source = slot_of(e)
        return target, source, jnp.where(value > 0, g[source].astype(jnp.float32), 0.0)

    def add_pairs(items):
        add_rows([t for t, _, _ in items], [half_pair(*item) for item in items])

    def early(*chips):
        add_pairs([chosen_block(c * NCORE + h) for c in chips for h in range(NCORE)])

    def both(c):
        to_partner(c).wait_recv()

    near = ((1, 0), (-1, 0), (0, 1), (0, -1))
    diag = ((1, 1), (1, -1), (-1, 1), (-1, -1))
    far = ((2, 0), (0, 2))
    knight = ((2, 1), (2, -1), (1, 2), (-1, 2))

    def forward(group):
        for dx, dz in group:
            to_partner(chip_at(dx, dz)).start()

    def near_factors(i):
        sign, along = 1 - 2 * lax.rem(i, 2), i // 2
        c = chip_at(sign * (1 - along), sign * along)
        both(c)
        add_factors(c)

    def diag_factors(i):
        c = chip_at(1 - 2 * (i // 2), 1 - 2 * lax.rem(i, 2))
        both(c)
        add_factors(c)

    def far_factors(i):
        c = chip_at(2 * (1 - i), 2 * i)
        both(c)
        add_factors(c)

    def knight_factors(i):
        sign, along = 1 - 2 * lax.rem(i, 2), i // 2
        c = chip_at(2 * (1 - along) + sign * along, sign * (1 - along) + 2 * along)
        both(c)
        add_factors(c)

    for i in range(3):
        table_x(i).wait_recv()
    for i in range(3):
        table_z(i).start()
    own.wait()
    own_out.wait_recv()
    add_factors(chip)
    arrived(0, 1)
    start(4, 5, 6, 7, 8, 9)
    arrived(2, 3)
    start(14, 15)
    forward(near)

    arrived(4, 7)
    start(10, 11, 12, 13)
    pl.loop(0, 4)(near_factors)
    for i in range(3):
        table_z(i).wait_recv()
    table_core.start()
    arrived(5, 6, 8, 9)
    start(16, 17, 18, 19)
    forward(diag)
    arrived(14, 15)
    forward(far)
    table_core.wait_recv()
    rows = table[...].reshape(NSPACE, 1, BLOCK) - me * (PER * BLOCK)
    hit = jnp.where((rows > 0) & (rows <= PER * BLOCK), rows, 0)
    codes[...] = jnp.broadcast_to(jnp.sum(hit, axis=2, keepdims=True), (NSPACE, 1, BLOCK))
    to_smem = pltpu.make_async_copy(codes, code_s, ls.at[2])
    to_smem.start()
    to_smem.wait()
    early(chip, chip_at(1, 0))
    arrived(10, 13)
    start(20, 21)
    early(chip_at(-1, 0), chip_at(0, 1))
    arrived(11, 12, 16, 17, 18, 19)
    forward(knight)
    pl.loop(0, 4)(diag_factors)
    pl.loop(0, 2)(far_factors)
    early(chip_at(0, -1), chip_at(1, 1))
    arrived(20, 21)
    forward(((2, 2),))
    pl.loop(0, 4)(knight_factors)
    early(chip_at(1, -1), chip_at(-1, 1))
    early(chip_at(2, 0), chip_at(0, 2))
    both(chip_at(2, 2))
    add_factors(chip_at(2, 2))

    n = [r[:, 0:1] for r in nrow]
    q = (2.0 * math.pi / 8.0) ** 2 * (n[0] * n[0] + n[1] * n[1] + n[2] * n[2])
    sm = smear[...]
    kern = (4.0 * math.pi / q) * jnp.exp(-0.5 * q * (sm * sm))
    fg[core, 0, x, z] = (s_acc[0:32, :] * kern).astype(jnp.bfloat16)
    fg[core, 1, x, z] = (s_acc[32:64, :] * kern).astype(jnp.bfloat16)

    def f_x(i):
        mine = fg.at[core, :, x, z]
        return remote(mine, mine, fs.at[i], fr.at[i], xpeers[i])

    def f_z(i):
        mine = fg.at[core, :, :, z]
        return remote(mine, mine, fs.at[3 + i], fr.at[3 + i], zpeers[i])

    f_core = remote(fg.at[core], fg.at[core], fs.at[6], fr.at[6], partner)
    for i in range(3):
        f_x(i).start()

    def late_step(i):
        late, last = i // 3, i // 5
        c = chip_at(2 * (1 - late) + late * (1 + 2 * (i - 3) - 2 * last), (1 - late) * (1 + i) + late * (2 + last))
        add_pairs([loaded_block(c * NCORE), loaded_block(c * NCORE + 1), own_slot(2 * i), own_slot(2 * i + 1)])

    pl.loop(0, 2)(late_step)
    for i in range(3):
        f_x(i).wait_recv()
    for i in range(3):
        f_z(i).start()
    pl.loop(2, 5)(late_step)
    for i in range(3):
        f_z(i).wait_recv()
    f_core.start()
    late_step(5)
    add_pairs([own_slot(s) for s in range(12, 16)])
    f_core.wait_recv()

    def message(b):
        at = pl.ds(b * BLOCK, BLOCK)
        recip = jnp.dot(cs[at, :], fg[...].reshape(2 * KV, CH), preferred_element_type=jnp.float32)
        recip = recip * (4.0 / math.sqrt(16384.0 * KV))
        m[yme, b] = (0.25 * acc[at, :] + recip).astype(jnp.bfloat16)

    def hop(i, origin, b, to):
        piece = m.at[origin, b]
        return pltpu.make_async_remote_copy(
            src_ref=piece, dst_ref=piece, send_sem=ms.at[i], recv_sem=mr.at[i],
            device_id={"chan": to}, device_id_type=MESH)

    ups = [hop(b, yme, b, yup) for b in range(PER)]
    downs = [hop(PER + b, yme, b, ydown) for b in range(PER)]
    relays = [hop(2 * PER + b, ydown, b, yup) for b in (0, 1)] + [hop(2 * PER + b, yup, b, ydown) for b in (2, 3)]
    message(0)
    message(2)
    ups[0].start()
    downs[2].start()
    message(1)
    message(3)
    ups[1].start()
    downs[3].start()
    ups[2].start()
    downs[0].start()
    ups[3].start()
    downs[1].start()

    def mixed(origin):
        rows = pl.ds(pl.multiple_of(origin * CH, CH), CH)
        return jnp.dot(m[origin].reshape(ROWS, CH), mix[rows, :], preferred_element_type=jnp.float32)

    ups[0].wait_recv()
    relays[0].start()
    downs[2].wait_recv()
    relays[2].start()
    ups[1].wait_recv()
    relays[1].start()
    downs[3].wait_recv()
    relays[3].start()
    total = feat[...].reshape(ROWS, CH).astype(jnp.float32) + mixed(yme)
    ups[2].wait_recv()
    ups[3].wait_recv()
    total = total + mixed(ydown)
    downs[0].wait_recv()
    downs[1].wait_recv()
    total = total + mixed(yup)
    for c in relays:
        c.wait_recv()
    out[...] = (total + mixed(yacross)).astype(jnp.bfloat16)

    for i in range(NEV):
        for flow in (0, 1):
            ev(flow, i).wait_send()
    own_out.wait_send()
    for c in ups + downs + relays:
        c.wait_send()

    for i in range(3):
        for c in (table_x(i), table_z(i), f_x(i), f_z(i)):
            c.wait_send()
    table_core.wait_send()
    f_core.wait_send()

    @pl.loop(1, NX * NZ)
    def _(i):
        to_partner(lax.rem(chip + i, NX * NZ)).wait_send()


def body(features, positions, pair_first, pair_second, pair_counts, wave_index,
         radial_weight, smearing, mix_weight):
    dma = pltpu.SemaphoreType.DMA
    bf16, f32 = jnp.bfloat16, jnp.float32
    return pl.pallas_call(
        kernel,
        out_shape=jax.ShapeDtypeStruct((ROWS, CH), bf16),
        in_specs=[VM, SM, SM, SM] + [VM] * 8,
        out_specs=VM,
        scratch_shapes=[
            pltpu.VMEM((NSPACE * PER, BLOCK, CH), bf16),
            pltpu.VMEM((NCORE, NX, NZ, 1, BLOCK), jnp.int32),
            pltpu.VMEM((NSPACE, 1, BLOCK), jnp.int32),
            pltpu.SMEM((NSPACE, 1, BLOCK), jnp.int32),
            pltpu.VMEM((NCORE, 2, NX, NZ, 32, CH), bf16),
            pltpu.VMEM((ROWS, 2 * KV), bf16),
            pltpu.VMEM((ROWS, CH), f32),
            pltpu.VMEM((3, PER, BLOCK, BLOCK), f32),
            pltpu.VMEM((NSPACE * PER, 3, BLOCK), f32),
            pltpu.VMEM((3, BLOCK, BLOCK), f32),
            pltpu.VMEM((NB, 16, CH), bf16),
            pltpu.VMEM((64, CH), f32),
            pltpu.VMEM((NCHAN, PER, BLOCK, CH), bf16),
            dma((2, NEV)), dma((2, NEV)),
            dma((7,)), dma((7,)),
            dma((NX * NZ + 1,)), dma((NX * NZ + 1,)),
            dma((7,)), dma((7,)),
            dma((3 * PER,)), dma((3 * PER,)),
            dma((3,)),
        ],
        compiler_params=pltpu.CompilerParams(collective_id=0, has_side_effects=True),
        name="layer",
    )(features.reshape(PER, BLOCK, CH), pair_first, pair_second, pair_counts, pair_first[None, :], pair_second[None, :],
      pair_counts[None, :], positions, wave_index, radial_weight, smearing[None, :], mix_weight)


def solution(mesh):
    placed = (P("space", "chan"), P(), P("space"), P("space"), P("space"), P(),
              P(None, "chan"), P("chan"), P(None, "chan"))
    return jax.shard_map(
        body, mesh=mesh, in_specs=placed, out_specs=P("space", "chan"), check_vma=False
    )
```

```python
import functools
import math

import jax
import jax.numpy as jnp
from jax import lax
from jax.experimental import pallas as pl
from jax.experimental.pallas import tpu as pltpu
from jax.sharding import PartitionSpec as P

BLOCK = 128
NX, NZ, NCORE, NCHAN = 4, 4, 2, 4
NSPACE = NX * NZ * NCORE
ROWS = 512
CH = 128
KV = 1024
NB = 32
MESH = pl.DeviceIdType.MESH
VM = pl.BlockSpec(memory_space=pltpu.VMEM)
SM = pl.BlockSpec(memory_space=pltpu.SMEM)

REACH = 4.0 * math.sqrt(3.0)
STEP = REACH / (NB - 1)
SPREAD = 1.5 * STEP
SCALE = math.sqrt(math.log2(math.e)) / SPREAD
DELTA = STEP * SCALE
GROUP = 8
PER = ROWS // BLOCK

SIN_C = (3.14159264, -5.167710084, 2.550077523, -0.5982912856, 0.0776576603)
COS_C = (0.9999999532, -4.934792831, 4.058411353, -1.331876568, 0.2196896111)


def horner(v, coeffs):
    out = coeffs[-1] * v + coeffs[-2]
    for c in coeffs[-3::-1]:
        out = out * v + c
    return out


def cos_sin_turns(t):
    u = t - jnp.floor(t + 0.5)
    v = u * u
    s = u * horner(v, SIN_C)
    c = horner(v, COS_C)
    s2 = s + s
    return (1.0 - s2 * s).astype(jnp.bfloat16), (s2 * c).astype(jnp.bfloat16)


def remote(src, dst, send, recv, space):
    return pltpu.make_async_remote_copy(
        src_ref=src, dst_ref=dst, send_sem=send, recv_sem=recv,
        device_id={"space": space}, device_id_type=MESH,
    )


def place(x, z, core):
    return (lax.rem(x + 2 * NX, NX) * NZ + lax.rem(z + 2 * NZ, NZ)) * NCORE + core


HALF = ROWS // 2
QUART = ROWS // 4
FULL, LO, HI = (0, HALF), (0, QUART), (QUART, QUART)
EVENTS = (
    (0, 0, FULL, 1, 0), (0, 0, FULL, -1, 0), (0, 0, FULL, 0, 1), (0, 0, FULL, 0, -1),
    (-1, 0, LO, 1, 0), (-1, 0, FULL, 0, 1), (-1, 0, FULL, 0, -1),
    (1, 0, HI, -1, 0), (1, 0, FULL, 0, 1), (1, 0, FULL, 0, -1),
    (-2, 0, LO, 0, 1), (-2, 0, LO, 0, -1), (2, 0, HI, 0, 1), (2, 0, HI, 0, -1),
    (0, -1, LO, 0, 1), (0, 1, HI, 0, -1),
    (-1, -1, LO, 0, 1), (-1, 1, HI, 0, -1), (1, -1, LO, 0, 1), (1, 1, HI, 0, -1),
    (-2, -1, LO, 0, 1), (2, 1, HI, 0, -1),
)
NEV = len(EVENTS)


def expansion(d2):
    out = [None] * NB
    half = GROUP // 2
    shrink = 1.0 / (4.0 * DELTA * DELTA)
    dk = d2 * shrink
    for c in range(half, NB, GROUP):
        centre = 2.0 * c * DELTA * DELTA
        a = d2 - centre
        mid = jnp.exp2(a * (centre * shrink - dk))
        up, down = jnp.exp2(a), jnp.exp2(centre - d2)
        out[c] = mid
        for sign, ratio, length in ((1, up, GROUP - half - 1), (-1, down, half)):
            e = mid
            for j in range(1, length + 1):
                if j == 3:
                    e, ratio = out[c + 2 * sign], ratio.astype(jnp.bfloat16)
                e = e * ratio
                out[c + sign * j] = e.astype(jnp.bfloat16)
        out[c] = mid.astype(jnp.bfloat16)
    return out


def kernel(feat, first, second, count, first_v, second_v, count_v, pos, wave, weight, smear, mix, out,
           g, table, codes, code_s, fg, cs, acc, posb, posq, wt, wb, s_acc, m,
           gs, gr, ks, kr, ps, pr, fs, fr, ms, mr, ls):
    me = lax.axis_index("space")
    yme = lax.axis_index("chan")
    core = lax.rem(me, NCORE)
    chip = me // NCORE
    x, z = chip // NZ, lax.rem(chip, NZ)
    partner = chip * NCORE + (1 - core)
    yup, ydown = lax.rem(yme + 1, NCHAN), lax.rem(yme + NCHAN - 1, NCHAN)
    yacross = lax.rem(yme + 2, NCHAN)

    barrier = pltpu.get_barrier_semaphore()

    xpeers = [place(x + i, z, core) for i in (1, 2, 3)]
    zpeers = [place(x, z + i, core) for i in (1, 2, 3)]
    for peer in xpeers + zpeers + [partner]:
        pl.semaphore_signal(barrier, inc=1, device_id={"space": peer}, device_id_type=MESH)
    for peer in (yup, ydown):
        pl.semaphore_signal(barrier, inc=1, device_id={"chan": peer}, device_id_type=MESH)

    own = pltpu.make_async_copy(feat, g.at[pl.ds(me * PER, PER)], ls.at[0])
    own.start()

    slot = lax.broadcasted_iota(jnp.int32, (1, 16), 1)
    listed = jnp.where(slot < count_v[...], first_v[...] + BLOCK * second_v[...] + 1, 0)
    table[core, x, z] = jnp.zeros((1, BLOCK), jnp.int32)
    table[core, x, z, :, 0:16] = listed

    pl.semaphore_wait(barrier, 9)

    def ev(flow, i):
        da, db, (r0, n), sa, sb = EVENTS[i]
        if flow == 0:
            origin, to = place(x + da, z + db, core), place(x + sa, z + sb, core)
        else:
            origin, to = place(x + db, z + da, core), place(x + sb, z + sa, core)
        first_row = (flow * HALF + r0) // BLOCK
        blocks = g.at[pl.ds(origin * PER + first_row, n // BLOCK)]
        src = feat.at[pl.ds(first_row, n // BLOCK)] if da == 0 and db == 0 else blocks
        return remote(src, blocks, gs.at[flow, i], gr.at[flow, i], to)

    def table_x(i):
        mine = table.at[core, x, z]
        return remote(mine, mine, ks.at[i], kr.at[i], xpeers[i])

    def table_z(i):
        mine = table.at[core, :, z]
        return remote(mine, mine, ks.at[3 + i], kr.at[3 + i], zpeers[i])

    table_core = remote(table.at[core], table.at[core], ks.at[6], kr.at[6], partner)

    def to_partner(c):
        blocks = g.at[pl.ds((c * NCORE + core) * PER, PER)]
        return remote(blocks, blocks, ps.at[c], pr.at[c], partner)

    def start(*events):
        for i in events:
            for flow in (0, 1):
                ev(flow, i).start()

    def arrived(*events):
        for i in events:
            for flow in (0, 1):
                ev(flow, i).wait_recv()

    def chip_at(dx, dz):
        return lax.rem(x + dx + NX, NX) * NZ + lax.rem(z + dz + NZ, NZ)

    for i in range(3):
        table_x(i).start()
    start(0, 1, 2, 3)
    own_out = remote(feat, g.at[pl.ds(me * PER, PER)], ps.at[NX * NZ], pr.at[NX * NZ], partner)
    own_out.start()

    for k in range(NB):
        j = k % GROUP - GROUP // 2
        row = weight[k:k + 1, :].astype(jnp.float32) * (2.0 ** (-j * j * DELTA * DELTA))
        wb[k] = jnp.broadcast_to(row, (16, CH)).astype(jnp.bfloat16)

    for a in range(3):
        for b in range(PER):
            at = pl.ds(pl.multiple_of(me * ROWS + b * BLOCK, BLOCK), BLOCK)
            posb[a, b] = jnp.broadcast_to(pos[a:a + 1, at], (BLOCK, BLOCK)).T
        at = pl.ds(pl.multiple_of(core * 512 + (chip // 4) * BLOCK, BLOCK), BLOCK)
        wt[a] = jnp.broadcast_to(wave[a:a + 1, at].astype(jnp.float32), (BLOCK, BLOCK)).T

    @pl.loop(0, NSPACE * PER // 8)
    def _(i):
        for j in range(8):
            at = pl.ds(pl.multiple_of(i * 1024 + j * BLOCK, BLOCK), BLOCK)
            posq[i * 8 + j] = pos[:, at]
    acc[...] = jnp.zeros_like(acc)
    s_acc[...] = jnp.zeros_like(s_acc)

    @pl.loop(0, PER)
    def _(b):
        at = pl.ds(pl.multiple_of(b * BLOCK, BLOCK), BLOCK)
        for h in range(NCORE):
            for part in range(2):
                k0 = h * 512 + part * 256
                t = None
                for a in range(3):
                    n = wave[a:a + 1, k0:k0 + 256].astype(jnp.float32)
                    p = posb[a, b]
                    term = jnp.concatenate([p, p], 1) * n
                    t = term if t is None else t + term
                c, s = cos_sin_turns(t * 0.125)
                col = h * 1024 + part * 256
                cs[at, col:col + 256] = c
                cs[at, col + 512:col + 768] = s

    mine = pl.ds(pl.multiple_of(lax.rem(chip, 4) * 32, 32), 32)
    nrow = [wt[a, mine, :] for a in range(3)]

    def distance(target, source):
        total = None
        there = posq[source]
        for a in range(3):
            off = jnp.abs(there[a:a + 1, :] - posb[a, target])
            off = jnp.minimum(off, 8.0 - off)
            total = off * off if total is None else total + off * off
        return jnp.sqrt(total) * (SCALE * 2.0 * DELTA)

    def half_pair(target, source, f32_rows):
        es = expansion(distance(target, source))
        f = f32_rows.astype(jnp.bfloat16).reshape(8, 16, CH)
        total = None
        for k in range(0, NB, 2):
            lhs = jnp.concatenate(es[k:k + 2], 1)
            rhs = jnp.concatenate([(f * wb[k + j][None]).reshape(BLOCK, CH) for j in range(2)], 0)
            part = jnp.dot(lhs, rhs, preferred_element_type=jnp.float32)
            total = part if total is None else total + part
        return total

    def add_rows(targets, values):
        for b in range(PER):
            rows = acc[b * BLOCK:(b + 1) * BLOCK, :]
            for target, value in zip(targets, values):
                rows = rows + jnp.where(target == b, value, 0.0)
            acc[b * BLOCK:(b + 1) * BLOCK, :] = rows

    def add_factors(c):
        at = [pl.ds(pl.multiple_of(c * 1024 + i * BLOCK, BLOCK), BLOCK) for i in range(8)]
        blocks = []
        for i in range(8):
            t = nrow[0] * pos[0:1, at[i]] + nrow[1] * pos[1:2, at[i]] + nrow[2] * pos[2:3, at[i]]
            co, si = cos_sin_turns(t * 0.125)
            blocks.append(jnp.concatenate([co, si], 0))
        rows = g[pl.ds(c * NCORE * PER, NCORE * PER)].reshape(NCORE * ROWS, CH)
        s_acc[...] += jnp.dot(jnp.concatenate(blocks, 1), rows, preferred_element_type=jnp.float32)

    def slot_of(e):
        value = code_s[lax.rem(e, NCORE) * (NX * NZ) + e // NCORE, 0, 0]
        v = jnp.maximum(value - 1, 0)
        return value, v // BLOCK, lax.rem(v, BLOCK)

    def own_slot(s):
        f = g[second[s]].astype(jnp.float32)
        return lax.rem(first[s], PER), second[s], jnp.where(s < count[0], f, 0.0)

    def chosen_block(e):
        value, target, source = slot_of(e)
        local = jnp.where(value > 0, source - e * PER, -1)
        f = jnp.zeros((BLOCK, CH), jnp.bfloat16)
        for b in range(PER):
            f = jnp.where(local == b, g[e * PER + b], f)
        return target, source, f.astype(jnp.float32)

    def loaded_block(e):
        value, target, source = slot_of(e)
        return target, source, jnp.where(value > 0, g[source].astype(jnp.float32), 0.0)

    def add_pairs(items):
        add_rows([t for t, _, _ in items], [half_pair(*item) for item in items])

    def early(*chips):
        add_pairs([chosen_block(c * NCORE + h) for c in chips for h in range(NCORE)])

    def both(c):
        to_partner(c).wait_recv()

    near = ((1, 0), (-1, 0), (0, 1), (0, -1))
    diag = ((1, 1), (1, -1), (-1, 1), (-1, -1))
    far = ((2, 0), (0, 2))
    knight = ((2, 1), (2, -1), (1, 2), (-1, 2))

    def forward(group):
        for dx, dz in group:
            to_partner(chip_at(dx, dz)).start()

    def near_factors(i):
        sign, along = 1 - 2 * lax.rem(i, 2), i // 2
        c = chip_at(sign * (1 - along), sign * along)
        both(c)
        add_factors(c)

    def diag_factors(i):
        c = chip_at(1 - 2 * (i // 2), 1 - 2 * lax.rem(i, 2))
        both(c)
        add_factors(c)

    def far_factors(i):
        c = chip_at(2 * (1 - i), 2 * i)
        both(c)
        add_factors(c)

    def knight_factors(i):
        sign, along = 1 - 2 * lax.rem(i, 2), i // 2
        c = chip_at(2 * (1 - along) + sign * along, sign * (1 - along) + 2 * along)
        both(c)
        add_factors(c)

    for i in range(3):
        table_x(i).wait_recv()
    for i in range(3):
        table_z(i).start()
    own.wait()
    own_out.wait_recv()
    add_factors(chip)
    arrived(0, 1)
    start(4, 5, 6, 7, 8, 9)
    arrived(2, 3)
    start(14, 15)
    forward(near)

    arrived(4, 7)
    start(10, 11, 12, 13)
    pl.loop(0, 4)(near_factors)
    for i in range(3):
        table_z(i).wait_recv()
    table_core.start()
    arrived(5, 6, 8, 9)
    start(16, 17, 18, 19)
    forward(diag)
    arrived(14, 15)
    forward(far)
    table_core.wait_recv()
    rows = table[...].reshape(NSPACE, 1, BLOCK) - me * (PER * BLOCK)
    hit = jnp.where((rows > 0) & (rows <= PER * BLOCK), rows, 0)
    codes[...] = jnp.broadcast_to(jnp.sum(hit, axis=2, keepdims=True), (NSPACE, 1, BLOCK))
    to_smem = pltpu.make_async_copy(codes, code_s, ls.at[2])
    to_smem.start()
    to_smem.wait()
    early(chip, chip_at(1, 0))
    arrived(10, 13)
    start(20, 21)
    early(chip_at(-1, 0), chip_at(0, 1))
    arrived(11, 12, 16, 17, 18, 19)
    forward(knight)
    pl.loop(0, 4)(diag_factors)
    pl.loop(0, 2)(far_factors)
    early(chip_at(0, -1), chip_at(1, 1))
    arrived(20, 21)
    forward(((2, 2),))
    pl.loop(0, 4)(knight_factors)
    early(chip_at(1, -1), chip_at(-1, 1))
    early(chip_at(2, 0), chip_at(0, 2))
    both(chip_at(2, 2))
    add_factors(chip_at(2, 2))

    n = [r[:, 0:1] for r in nrow]
    q = (2.0 * math.pi / 8.0) ** 2 * (n[0] * n[0] + n[1] * n[1] + n[2] * n[2])
    sm = smear[...]
    kern = (4.0 * math.pi / q) * jnp.exp(-0.5 * q * (sm * sm))
    fg[core, 0, x, z] = (s_acc[0:32, :] * kern).astype(jnp.bfloat16)
    fg[core, 1, x, z] = (s_acc[32:64, :] * kern).astype(jnp.bfloat16)

    def f_x(i):
        mine = fg.at[core, :, x, z]
        return remote(mine, mine, fs.at[i], fr.at[i], xpeers[i])

    def f_z(i):
        mine = fg.at[core, :, :, z]
        return remote(mine, mine, fs.at[3 + i], fr.at[3 + i], zpeers[i])

    f_core = remote(fg.at[core], fg.at[core], fs.at[6], fr.at[6], partner)
    for i in range(3):
        f_x(i).start()

    def late_step(i):
        late, last = i // 3, i // 5
        c = chip_at(2 * (1 - late) + late * (1 + 2 * (i - 3) - 2 * last), (1 - late) * (1 + i) + late * (2 + last))
        add_pairs([loaded_block(c * NCORE), loaded_block(c * NCORE + 1), own_slot(2 * i), own_slot(2 * i + 1)])

    pl.loop(0, 2)(late_step)
    for i in range(3):
        f_x(i).wait_recv()
    for i in range(3):
        f_z(i).start()
    pl.loop(2, 5)(late_step)
    for i in range(3):
        f_z(i).wait_recv()
    f_core.start()
    late_step(5)
    add_pairs([own_slot(s) for s in range(12, 16)])
    f_core.wait_recv()

    def message(b):
        at = pl.ds(b * BLOCK, BLOCK)
        recip = jnp.dot(cs[at, :], fg[...].reshape(2 * KV, CH), preferred_element_type=jnp.float32)
        recip = recip * (4.0 / math.sqrt(16384.0 * KV))
        m[yme, b] = (0.25 * acc[at, :] + recip).astype(jnp.bfloat16)

    def hop(i, origin, b, to):
        piece = m.at[origin, b]
        return pltpu.make_async_remote_copy(
            src_ref=piece, dst_ref=piece, send_sem=ms.at[i], recv_sem=mr.at[i],
            device_id={"chan": to}, device_id_type=MESH)

    ups = [hop(b, yme, b, yup) for b in range(PER)]
    downs = [hop(PER + b, yme, b, ydown) for b in range(PER)]
    relays = [hop(2 * PER + b, ydown, b, yup) for b in (0, 1)] + [hop(2 * PER + b, yup, b, ydown) for b in (2, 3)]
    message(0)
    message(2)
    ups[0].start()
    downs[2].start()
    message(1)
    message(3)
    ups[1].start()
    downs[3].start()
    ups[2].start()
    downs[0].start()
    ups[3].start()
    downs[1].start()

    def mixed(origin):
        rows = pl.ds(pl.multiple_of(origin * CH, CH), CH)
        return jnp.dot(m[origin].reshape(ROWS, CH), mix[rows, :], preferred_element_type=jnp.float32)

    ups[0].wait_recv()
    relays[0].start()
    downs[2].wait_recv()
    relays[2].start()
    ups[1].wait_recv()
    relays[1].start()
    downs[3].wait_recv()
    relays[3].start()
    total = feat[...].reshape(ROWS, CH).astype(jnp.float32) + mixed(yme)
    ups[2].wait_recv()
    ups[3].wait_recv()
    total = total + mixed(ydown)
    downs[0].wait_recv()
    downs[1].wait_recv()
    total = total + mixed(yup)
    for c in relays:
        c.wait_recv()
    out[...] = (total + mixed(yacross)).astype(jnp.bfloat16)

    for i in range(NEV):
        for flow in (0, 1):
            ev(flow, i).wait_send()
    own_out.wait_send()
    for c in ups + downs + relays:
        c.wait_send()

    for i in range(3):
        for c in (table_x(i), table_z(i), f_x(i), f_z(i)):
            c.wait_send()
    table_core.wait_send()
    f_core.wait_send()

    @pl.loop(1, NX * NZ)
    def _(i):
        to_partner(lax.rem(chip + i, NX * NZ)).wait_send()


def body(features, positions, pair_first, pair_second, pair_counts, wave_index,
         radial_weight, smearing, mix_weight):
    dma = pltpu.SemaphoreType.DMA
    bf16, f32 = jnp.bfloat16, jnp.float32
    return pl.pallas_call(
        kernel,
        out_shape=jax.ShapeDtypeStruct((ROWS, CH), bf16),
        in_specs=[VM, SM, SM, SM] + [VM] * 8,
        out_specs=VM,
        scratch_shapes=[
            pltpu.VMEM((NSPACE * PER, BLOCK, CH), bf16),
            pltpu.VMEM((NCORE, NX, NZ, 1, BLOCK), jnp.int32),
            pltpu.VMEM((NSPACE, 1, BLOCK), jnp.int32),
            pltpu.SMEM((NSPACE, 1, BLOCK), jnp.int32),
            pltpu.VMEM((NCORE, 2, NX, NZ, 32, CH), bf16),
            pltpu.VMEM((ROWS, 2 * KV), bf16),
            pltpu.VMEM((ROWS, CH), f32),
            pltpu.VMEM((3, PER, BLOCK, BLOCK), f32),
            pltpu.VMEM((NSPACE * PER, 3, BLOCK), f32),
            pltpu.VMEM((3, BLOCK, BLOCK), f32),
            pltpu.VMEM((NB, 16, CH), bf16),
            pltpu.VMEM((64, CH), f32),
            pltpu.VMEM((NCHAN, PER, BLOCK, CH), bf16),
            dma((2, NEV)), dma((2, NEV)),
            dma((7,)), dma((7,)),
            dma((NX * NZ + 1,)), dma((NX * NZ + 1,)),
            dma((7,)), dma((7,)),
            dma((3 * PER,)), dma((3 * PER,)),
            dma((3,)),
        ],
        compiler_params=pltpu.CompilerParams(collective_id=0, has_side_effects=True),
        name="layer",
    )(features.reshape(PER, BLOCK, CH), pair_first, pair_second, pair_counts, pair_first[None, :], pair_second[None, :],
      pair_counts[None, :], positions, wave_index, radial_weight, smearing[None, :], mix_weight)


def solution(mesh):
    placed = (P("space", "chan"), P(), P("space"), P("space"), P("space"), P(),
              P(None, "chan"), P("chan"), P(None, "chan"))
    return jax.shard_map(
        body, mesh=mesh, in_specs=placed, out_specs=P("space", "chan"), check_vma=False
    )
```

```python
import functools
import math

import jax
import jax.numpy as jnp
from jax import lax
from jax.experimental import pallas as pl
from jax.experimental.pallas import tpu as pltpu
from jax.sharding import PartitionSpec as P

BLOCK = 128
NX, NZ, NCORE, NCHAN = 4, 4, 2, 4
NSPACE = NX * NZ * NCORE
ROWS = 512
CH = 128
KV = 1024
NB = 32
MESH = pl.DeviceIdType.MESH
VM = pl.BlockSpec(memory_space=pltpu.VMEM)
SM = pl.BlockSpec(memory_space=pltpu.SMEM)

REACH = 4.0 * math.sqrt(3.0)
STEP = REACH / (NB - 1)
SPREAD = 1.5 * STEP
SCALE = math.sqrt(math.log2(math.e)) / SPREAD
DELTA = STEP * SCALE
GROUP = 8
PER = ROWS // BLOCK

SIN_C = (3.14159264, -5.167710084, 2.550077523, -0.5982912856, 0.0776576603)
COS_C = (0.9999999532, -4.934792831, 4.058411353, -1.331876568, 0.2196896111)


def horner(v, coeffs):
    out = coeffs[-1] * v + coeffs[-2]
    for c in coeffs[-3::-1]:
        out = out * v + c
    return out


def cos_sin_turns(t):
    u = t - jnp.floor(t + 0.5)
    v = u * u
    s = u * horner(v, SIN_C)
    c = horner(v, COS_C)
    s2 = s + s
    return (1.0 - s2 * s).astype(jnp.bfloat16), (s2 * c).astype(jnp.bfloat16)


def remote(src, dst, send, recv, space):
    return pltpu.make_async_remote_copy(
        src_ref=src, dst_ref=dst, send_sem=send, recv_sem=recv,
        device_id={"space": space}, device_id_type=MESH,
    )


def place(x, z, core):
    return (lax.rem(x + 2 * NX, NX) * NZ + lax.rem(z + 2 * NZ, NZ)) * NCORE + core


HALF = ROWS // 2
QUART = ROWS // 4
FULL, LO, HI = (0, HALF), (0, QUART), (QUART, QUART)
EVENTS = (
    (0, 0, FULL, 1, 0), (0, 0, FULL, -1, 0), (0, 0, FULL, 0, 1), (0, 0, FULL, 0, -1),
    (-1, 0, LO, 1, 0), (-1, 0, FULL, 0, 1), (-1, 0, FULL, 0, -1),
    (1, 0, HI, -1, 0), (1, 0, FULL, 0, 1), (1, 0, FULL, 0, -1),
    (-2, 0, LO, 0, 1), (-2, 0, LO, 0, -1), (2, 0, HI, 0, 1), (2, 0, HI, 0, -1),
    (0, -1, LO, 0, 1), (0, 1, HI, 0, -1),
    (-1, -1, LO, 0, 1), (-1, 1, HI, 0, -1), (1, -1, LO, 0, 1), (1, 1, HI, 0, -1),
    (-2, -1, LO, 0, 1), (2, 1, HI, 0, -1),
)
NEV = len(EVENTS)


def expansion(d2):
    out = [None] * NB
    half = GROUP // 2
    shrink = 1.0 / (4.0 * DELTA * DELTA)
    dk = d2 * shrink
    for c in range(half, NB, GROUP):
        centre = 2.0 * c * DELTA * DELTA
        a = d2 - centre
        mid = jnp.exp2(a * (centre * shrink - dk))
        up, down = jnp.exp2(a), jnp.exp2(centre - d2)
        out[c] = mid
        for sign, ratio, length in ((1, up, GROUP - half - 1), (-1, down, half)):
            e = mid
            for j in range(1, length + 1):
                if j == 2:
                    e, ratio = out[c + sign], ratio.astype(jnp.bfloat16)
                e = e * ratio
                out[c + sign * j] = e.astype(jnp.bfloat16)
        out[c] = mid.astype(jnp.bfloat16)
    return out


def kernel(feat, first, second, count, first_v, second_v, count_v, pos, wave, weight, smear, mix, out,
           g, table, codes, code_s, fg, cs, acc, posb, posq, wt, wb, s_acc, m,
           gs, gr, ks, kr, ps, pr, fs, fr, ms, mr, ls):
    me = lax.axis_index("space")
    yme = lax.axis_index("chan")
    core = lax.rem(me, NCORE)
    chip = me // NCORE
    x, z = chip // NZ, lax.rem(chip, NZ)
    partner = chip * NCORE + (1 - core)
    yup, ydown = lax.rem(yme + 1, NCHAN), lax.rem(yme + NCHAN - 1, NCHAN)
    yacross = lax.rem(yme + 2, NCHAN)

    barrier = pltpu.get_barrier_semaphore()

    xpeers = [place(x + i, z, core) for i in (1, 2, 3)]
    zpeers = [place(x, z + i, core) for i in (1, 2, 3)]
    for peer in xpeers + zpeers + [partner]:
        pl.semaphore_signal(barrier, inc=1, device_id={"space": peer}, device_id_type=MESH)
    for peer in (yup, ydown):
        pl.semaphore_signal(barrier, inc=1, device_id={"chan": peer}, device_id_type=MESH)

    own = pltpu.make_async_copy(feat, g.at[pl.ds(me * PER, PER)], ls.at[0])
    own.start()

    slot = lax.broadcasted_iota(jnp.int32, (1, 16), 1)
    listed = jnp.where(slot < count_v[...], first_v[...] + BLOCK * second_v[...] + 1, 0)
    table[core, x, z] = jnp.zeros((1, BLOCK), jnp.int32)
    table[core, x, z, :, 0:16] = listed

    for k in range(NB):
        j = k % GROUP - GROUP // 2
        row = weight[k:k + 1, :].astype(jnp.float32) * (2.0 ** (-j * j * DELTA * DELTA))
        wb[k] = jnp.broadcast_to(row, (16, CH)).astype(jnp.bfloat16)

    pl.semaphore_wait(barrier, 9)

    def ev(flow, i):
        da, db, (r0, n), sa, sb = EVENTS[i]
        if flow == 0:
            origin, to = place(x + da, z + db, core), place(x + sa, z + sb, core)
        else:
            origin, to = place(x + db, z + da, core), place(x + sb, z + sa, core)
        first_row = (flow * HALF + r0) // BLOCK
        blocks = g.at[pl.ds(origin * PER + first_row, n // BLOCK)]
        src = feat.at[pl.ds(first_row, n // BLOCK)] if da == 0 and db == 0 else blocks
        return remote(src, blocks, gs.at[flow, i], gr.at[flow, i], to)

    def table_x(i):
        mine = table.at[core, x, z]
        return remote(mine, mine, ks.at[i], kr.at[i], xpeers[i])

    def table_z(i):
        mine = table.at[core, :, z]
        return remote(mine, mine, ks.at[3 + i], kr.at[3 + i], zpeers[i])

    table_core = remote(table.at[core], table.at[core], ks.at[6], kr.at[6], partner)

    def to_partner(c):
        blocks = g.at[pl.ds((c * NCORE + core) * PER, PER)]
        return remote(blocks, blocks, ps.at[c], pr.at[c], partner)

    def start(*events):
        for i in events:
            for flow in (0, 1):
                ev(flow, i).start()

    def arrived(*events):
        for i in events:
            for flow in (0, 1):
                ev(flow, i).wait_recv()

    def chip_at(dx, dz):
        return lax.rem(x + dx + NX, NX) * NZ + lax.rem(z + dz + NZ, NZ)

    for i in range(3):
        table_x(i).start()
    start(0, 1, 2, 3)
    own_out = remote(feat, g.at[pl.ds(me * PER, PER)], ps.at[NX * NZ], pr.at[NX * NZ], partner)
    own_out.start()

    for a in range(3):
        for b in range(PER):
            at = pl.ds(pl.multiple_of(me * ROWS + b * BLOCK, BLOCK), BLOCK)
            posb[a, b] = jnp.broadcast_to(pos[a:a + 1, at], (BLOCK, BLOCK)).T
        at = pl.ds(pl.multiple_of(core * 512 + (chip // 4) * BLOCK, BLOCK), BLOCK)
        wt[a] = jnp.broadcast_to(wave[a:a + 1, at].astype(jnp.float32), (BLOCK, BLOCK)).T

    @pl.loop(0, NSPACE * PER // 8)
    def _(i):
        for j in range(8):
            at = pl.ds(pl.multiple_of(i * 1024 + j * BLOCK, BLOCK), BLOCK)
            posq[i * 8 + j] = pos[:, at]
    acc[...] = jnp.zeros_like(acc)
    s_acc[...] = jnp.zeros_like(s_acc)

    @pl.loop(0, PER)
    def _(b):
        at = pl.ds(pl.multiple_of(b * BLOCK, BLOCK), BLOCK)
        for h in range(NCORE):
            for part in range(2):
                k0 = h * 512 + part * 256
                t = None
                for a in range(3):
                    n = wave[a:a + 1, k0:k0 + 256].astype(jnp.float32)
                    p = posb[a, b]
                    term = jnp.concatenate([p, p], 1) * n
                    t = term if t is None else t + term
                c, s = cos_sin_turns(t * 0.125)
                col = h * 1024 + part * 256
                cs[at, col:col + 256] = c
                cs[at, col + 512:col + 768] = s

    mine = pl.ds(pl.multiple_of(lax.rem(chip, 4) * 32, 32), 32)
    nrow = [wt[a, mine, :] for a in range(3)]

    def distance(target, source):
        total = None
        there = posq[source]
        for a in range(3):
            off = jnp.abs(there[a:a + 1, :] - posb[a, target])
            off = jnp.minimum(off, 8.0 - off)
            total = off * off if total is None else total + off * off
        return jnp.sqrt(total) * (SCALE * 2.0 * DELTA)

    def half_pair(target, source, f32_rows):
        es = expansion(distance(target, source))
        f = f32_rows.astype(jnp.bfloat16).reshape(8, 16, CH)
        total = None
        for k in range(0, NB, 2):
            lhs = jnp.concatenate(es[k:k + 2], 1)
            rhs = jnp.concatenate([(f * wb[k + j][None]).reshape(BLOCK, CH) for j in range(2)], 0)
            part = jnp.dot(lhs, rhs, preferred_element_type=jnp.float32)
            total = part if total is None else total + part
        return total

    def add_rows(targets, values):
        for b in range(PER):
            rows = acc[b * BLOCK:(b + 1) * BLOCK, :]
            for target, value in zip(targets, values):
                rows = rows + jnp.where(target == b, value, 0.0)
            acc[b * BLOCK:(b + 1) * BLOCK, :] = rows

    def add_factors(c):
        at = [pl.ds(pl.multiple_of(c * 1024 + i * BLOCK, BLOCK), BLOCK) for i in range(8)]
        blocks = []
        for i in range(8):
            t = nrow[0] * pos[0:1, at[i]] + nrow[1] * pos[1:2, at[i]] + nrow[2] * pos[2:3, at[i]]
            co, si = cos_sin_turns(t * 0.125)
            blocks.append(jnp.concatenate([co, si], 0))
        rows = g[pl.ds(c * NCORE * PER, NCORE * PER)].reshape(NCORE * ROWS, CH)
        s_acc[...] += jnp.dot(jnp.concatenate(blocks, 1), rows, preferred_element_type=jnp.float32)

    def slot_of(e):
        value = code_s[lax.rem(e, NCORE) * (NX * NZ) + e // NCORE, 0, 0]
        v = jnp.maximum(value - 1, 0)
        return value, v // BLOCK, lax.rem(v, BLOCK)

    def own_slot(s):
        f = g[second[s]].astype(jnp.float32)
        return lax.rem(first[s], PER), second[s], jnp.where(s < count[0], f, 0.0)

    def chosen_block(e):
        value, target, source = slot_of(e)
        local = jnp.where(value > 0, source - e * PER, -1)
        f = jnp.zeros((BLOCK, CH), jnp.bfloat16)
        for b in range(PER):
            f = jnp.where(local == b, g[e * PER + b], f)
        return target, source, f.astype(jnp.float32)

    def loaded_block(e):
        value, target, source = slot_of(e)
        return target, source, jnp.where(value > 0, g[source].astype(jnp.float32), 0.0)

    def add_pairs(items):
        add_rows([t for t, _, _ in items], [half_pair(*item) for item in items])

    def early(*chips):
        add_pairs([chosen_block(c * NCORE + h) for c in chips for h in range(NCORE)])

    def both(c):
        to_partner(c).wait_recv()

    near = ((1, 0), (-1, 0), (0, 1), (0, -1))
    diag = ((1, 1), (1, -1), (-1, 1), (-1, -1))
    far = ((2, 0), (0, 2))
    knight = ((2, 1), (2, -1), (1, 2), (-1, 2))

    def forward(group):
        for dx, dz in group:
            to_partner(chip_at(dx, dz)).start()

    def near_factors(i):
        sign, along = 1 - 2 * lax.rem(i, 2), i // 2
        c = chip_at(sign * (1 - along), sign * along)
        both(c)
        add_factors(c)

    def diag_factors(i):
        c = chip_at(1 - 2 * (i // 2), 1 - 2 * lax.rem(i, 2))
        both(c)
        add_factors(c)

    def far_factors(i):
        c = chip_at(2 * (1 - i), 2 * i)
        both(c)
        add_factors(c)

    def knight_factors(i):
        sign, along = 1 - 2 * lax.rem(i, 2), i // 2
        c = chip_at(2 * (1 - along) + sign * along, sign * (1 - along) + 2 * along)
        both(c)
        add_factors(c)

    for i in range(3):
        table_x(i).wait_recv()
    for i in range(3):
        table_z(i).start()
    own.wait()
    own_out.wait_recv()
    add_factors(chip)
    arrived(0, 1)
    start(4, 5, 6, 7, 8, 9)
    arrived(2, 3)
    start(14, 15)
    forward(near)

    arrived(4, 7)
    start(10, 11, 12, 13)
    pl.loop(0, 4)(near_factors)
    for i in range(3):
        table_z(i).wait_recv()
    table_core.start()
    arrived(5, 6, 8, 9)
    start(16, 17, 18, 19)
    forward(diag)
    arrived(14, 15)
    forward(far)
    table_core.wait_recv()
    rows = table[...].reshape(NSPACE, 1, BLOCK) - me * (PER * BLOCK)
    hit = jnp.where((rows > 0) & (rows <= PER * BLOCK), rows, 0)
    codes[...] = jnp.broadcast_to(jnp.sum(hit, axis=2, keepdims=True), (NSPACE, 1, BLOCK))
    to_smem = pltpu.make_async_copy(codes, code_s, ls.at[2])
    to_smem.start()
    to_smem.wait()
    early(chip, chip_at(1, 0))
    arrived(10, 13)
    start(20, 21)
    early(chip_at(-1, 0), chip_at(0, 1))
    arrived(11, 12, 16, 17, 18, 19)
    forward(knight)
    pl.loop(0, 4)(diag_factors)
    pl.loop(0, 2)(far_factors)
    early(chip_at(0, -1), chip_at(1, 1))
    arrived(20, 21)
    forward(((2, 2),))
    pl.loop(0, 4)(knight_factors)
    early(chip_at(1, -1), chip_at(-1, 1))
    early(chip_at(2, 0), chip_at(0, 2))
    both(chip_at(2, 2))
    add_factors(chip_at(2, 2))

    n = [r[:, 0:1] for r in nrow]
    q = (2.0 * math.pi / 8.0) ** 2 * (n[0] * n[0] + n[1] * n[1] + n[2] * n[2])
    sm = smear[...]
    kern = (4.0 * math.pi / q) * jnp.exp(-0.5 * q * (sm * sm))
    fg[core, 0, x, z] = (s_acc[0:32, :] * kern).astype(jnp.bfloat16)
    fg[core, 1, x, z] = (s_acc[32:64, :] * kern).astype(jnp.bfloat16)

    def f_x(i):
        mine = fg.at[core, :, x, z]
        return remote(mine, mine, fs.at[i], fr.at[i], xpeers[i])

    def f_z(i):
        mine = fg.at[core, :, :, z]
        return remote(mine, mine, fs.at[3 + i], fr.at[3 + i], zpeers[i])

    f_core = remote(fg.at[core], fg.at[core], fs.at[6], fr.at[6], partner)
    for i in range(3):
        f_x(i).start()

    def late_step(i):
        late, last = i // 3, i // 5
        c = chip_at(2 * (1 - late) + late * (1 + 2 * (i - 3) - 2 * last), (1 - late) * (1 + i) + late * (2 + last))
        add_pairs([loaded_block(c * NCORE), loaded_block(c * NCORE + 1), own_slot(2 * i), own_slot(2 * i + 1)])

    pl.loop(0, 2)(late_step)
    for i in range(3):
        f_x(i).wait_recv()
    for i in range(3):
        f_z(i).start()
    pl.loop(2, 5)(late_step)
    for i in range(3):
        f_z(i).wait_recv()
    f_core.start()
    late_step(5)
    add_pairs([own_slot(s) for s in range(12, 16)])
    f_core.wait_recv()

    def message(b):
        at = pl.ds(b * BLOCK, BLOCK)
        recip = jnp.dot(cs[at, :], fg[...].reshape(2 * KV, CH), preferred_element_type=jnp.float32)
        recip = recip * (4.0 / math.sqrt(16384.0 * KV))
        m[yme, b] = (0.25 * acc[at, :] + recip).astype(jnp.bfloat16)

    def hop(i, origin, b, to):
        piece = m.at[origin, b]
        return pltpu.make_async_remote_copy(
            src_ref=piece, dst_ref=piece, send_sem=ms.at[i], recv_sem=mr.at[i],
            device_id={"chan": to}, device_id_type=MESH)

    ups = [hop(b, yme, b, yup) for b in range(PER)]
    downs = [hop(PER + b, yme, b, ydown) for b in range(PER)]
    relays = [hop(2 * PER + b, ydown, b, yup) for b in (0, 1)] + [hop(2 * PER + b, yup, b, ydown) for b in (2, 3)]
    message(0)
    message(2)
    ups[0].start()
    downs[2].start()
    message(1)
    message(3)
    ups[1].start()
    downs[3].start()
    ups[2].start()
    downs[0].start()
    ups[3].start()
    downs[1].start()

    def mixed(origin):
        rows = pl.ds(pl.multiple_of(origin * CH, CH), CH)
        return jnp.dot(m[origin].reshape(ROWS, CH), mix[rows, :], preferred_element_type=jnp.float32)

    ups[0].wait_recv()
    relays[0].start()
    downs[2].wait_recv()
    relays[2].start()
    ups[1].wait_recv()
    relays[1].start()
    downs[3].wait_recv()
    relays[3].start()
    total = feat[...].reshape(ROWS, CH).astype(jnp.float32) + mixed(yme)
    ups[2].wait_recv()
    ups[3].wait_recv()
    total = total + mixed(ydown)
    downs[0].wait_recv()
    downs[1].wait_recv()
    total = total + mixed(yup)
    for c in relays:
        c.wait_recv()
    out[...] = (total + mixed(yacross)).astype(jnp.bfloat16)

    for i in range(NEV):
        for flow in (0, 1):
            ev(flow, i).wait_send()
    own_out.wait_send()
    for c in ups + downs + relays:
        c.wait_send()

    for i in range(3):
        for c in (table_x(i), table_z(i), f_x(i), f_z(i)):
            c.wait_send()
    table_core.wait_send()
    f_core.wait_send()

    @pl.loop(1, NX * NZ)
    def _(i):
        to_partner(lax.rem(chip + i, NX * NZ)).wait_send()


def body(features, positions, pair_first, pair_second, pair_counts, wave_index,
         radial_weight, smearing, mix_weight):
    dma = pltpu.SemaphoreType.DMA
    bf16, f32 = jnp.bfloat16, jnp.float32
    return pl.pallas_call(
        kernel,
        out_shape=jax.ShapeDtypeStruct((ROWS, CH), bf16),
        in_specs=[VM, SM, SM, SM] + [VM] * 8,
        out_specs=VM,
        scratch_shapes=[
            pltpu.VMEM((NSPACE * PER, BLOCK, CH), bf16),
            pltpu.VMEM((NCORE, NX, NZ, 1, BLOCK), jnp.int32),
            pltpu.VMEM((NSPACE, 1, BLOCK), jnp.int32),
            pltpu.SMEM((NSPACE, 1, BLOCK), jnp.int32),
            pltpu.VMEM((NCORE, 2, NX, NZ, 32, CH), bf16),
            pltpu.VMEM((ROWS, 2 * KV), bf16),
            pltpu.VMEM((ROWS, CH), f32),
            pltpu.VMEM((3, PER, BLOCK, BLOCK), f32),
            pltpu.VMEM((NSPACE * PER, 3, BLOCK), f32),
            pltpu.VMEM((3, BLOCK, BLOCK), f32),
            pltpu.VMEM((NB, 16, CH), bf16),
            pltpu.VMEM((64, CH), f32),
            pltpu.VMEM((NCHAN, PER, BLOCK, CH), bf16),
            dma((2, NEV)), dma((2, NEV)),
            dma((7,)), dma((7,)),
            dma((NX * NZ + 1,)), dma((NX * NZ + 1,)),
            dma((7,)), dma((7,)),
            dma((3 * PER,)), dma((3 * PER,)),
            dma((3,)),
        ],
        compiler_params=pltpu.CompilerParams(collective_id=0, has_side_effects=True),
        name="layer",
    )(features.reshape(PER, BLOCK, CH), pair_first, pair_second, pair_counts, pair_first[None, :], pair_second[None, :],
      pair_counts[None, :], positions, wave_index, radial_weight, smearing[None, :], mix_weight)


def solution(mesh):
    placed = (P("space", "chan"), P(), P("space"), P("space"), P("space"), P(),
              P(None, "chan"), P("chan"), P(None, "chan"))
    return jax.shard_map(
        body, mesh=mesh, in_specs=placed, out_specs=P("space", "chan"), check_vma=False
    )
```
